32 devices in a mesh: parts: 2 (over y), rows: 4 (over z), ex: 4 (over x, core).
Axes of the slice: x: 2, y: 2, z: 4, core: 2. Of those that a mesh axis runs over, the one named last changes fastest.
Arguments:
- hidden_acts: bfloat16 [1024, 512], P(('parts', 'ex'), 'rows'), parts along dimension 0, may hold values from -6 to 6
- cotangent: bfloat16 [1024, 4096], P(('parts', 'ex'), 'rows'), parts along dimension 0, may hold values from -0.796875 to 0.796875
- lengths: int32 [64], P('parts'), parts along dimension 0, may hold values from 1 to 64, 512 in all
- row_signs: int32 [512], P('rows'), may hold values from -1 to 1, as said below
- col_signs: int32 [4096], replicated, may hold values from -1 to 1, as said below
- feat_row: int32 [8192], replicated, may hold values from 0 to 511
- feat_col: int32 [8192], replicated, may hold values from 0 to 4095
- inverse_rows: bfloat16 [8192, 8192], P('rows'), as said below
Outputs:
- scores: bfloat16 [64, 8192], P(('parts', 'ex'), 'rows'), parts along dimension 0
The draws below stay inside these ranges and needn't reach their ends.
There are 2 independent parts, one for each index of `parts`. The reference program is written for one: setup_inputs(seed, part) draws one part's arguments, and reference() takes and returns one part's arrays. A program takes and returns all parts, laid end to end along the dimension named above; an argument that names none is the same for every part. Nothing has to cross between parts.
Inputs may be any that keep to these rules, and one draw needn't show every extreme that they name: `row_signs`: every entry is -1 or +1. `col_signs`: every entry is -1 or +1. `inverse_rows`: the whole matrix equals its transpose. The lengths sum to 512 and the largest equals 64.
All inputs are finite; a program needn't handle non-finite values.
Results may differ from the reference program's by a relative error of at most 0.0049.
Values may be sent and summed in bfloat16 or wider, within the bound.
A program may use at most 128 MiB of HBM per device.

```python
import math
import jax
import jax.numpy as jnp
import numpy as np
from jax import lax

D = 4096
FFW_DEV = 128
FFW = 512
K = 8192
EXAMPLES = 32
TOKENS = 512
MOST = 64
N_ROWS = 4


def draw_row_signs(key, part):
    return (2 * jax.random.randint(key, (FFW,), 0, 2) - 1).astype(jnp.int32)


def draw_col_signs(key, part):
    return (2 * jax.random.randint(key, (D,), 0, 2) - 1).astype(jnp.int32)


def draw_inverse_rows(key, part):
    base = jax.random.normal(key, (K, K), jnp.float32)
    mixed = (base + base.T) / jnp.sqrt(2.0 * K)
    weight = 0.3
    return (jnp.eye(K, dtype=jnp.float32) + weight * mixed).astype(jnp.bfloat16)


def place_ends(values, stream_key, smallest, high):
    dims = values.shape
    spot = [jax.random.randint(jax.random.fold_in(stream_key, axis), (), 0, dims[axis]) for axis in range(len(dims))]
    values = values.at[tuple(spot)].set(smallest)
    longest = dims.index(max(dims))
    spot[longest] = (spot[longest] + 1) % dims[longest]
    return values.at[tuple(spot)].set(high)


def levels(key, extent, split, smallest, largest):
    level = 1.0
    for dim, shards_of in split:
        heights = jax.random.uniform(jax.random.fold_in(jax.random.fold_in(key, 6), dim), (shards_of,), jnp.float32, smallest / len(split), largest / len(split))
        level = level * jnp.repeat(jnp.exp(heights), extent[dim] // shards_of).reshape((-1,) + (1,) * (len(extent) - 1 - dim))
    return level


def split_up(number_of, total, most, lean):
    portions = [(1 << 20) // math.isqrt(standing ** lean) + 1 for standing in range(2, number_of + 1)]
    rest, counts = total - most - (number_of - 1), [1] * (number_of - 1)
    while rest > 0:
        free = [i for i in range(number_of - 1) if counts[i] < most]
        pool, left = sum([portions[i] for i in free]), rest
        for i in free:
            more = min(most - counts[i], max(1, left * portions[i] // pool), rest)
            counts[i] = counts[i] + more
            rest = rest - more
    return np.array([most] + counts)


def ragged_sizes(own_key, number_of, total, most, lean):
    if number_of == 2:
        one = jax.random.randint(own_key, (), max(1, total - most), min(most, total - 1) + 1)
        return jnp.stack([one, total - one])
    sizes = jnp.asarray(split_up(number_of, total, most, lean), jnp.int32)
    twos = (number_of - 1) // 2
    source_of, sink = sizes[1:1 + 2 * twos:2], sizes[2:2 + 2 * twos:2]
    room = jnp.minimum(source_of - 1, most - sink)
    shifted = jax.random.randint(jax.random.fold_in(own_key, 1), (twos,), 0, 1 << 20) % (room + 1)
    sizes = sizes.at[1:1 + 2 * twos:2].set(source_of - shifted).at[2:2 + 2 * twos:2].set(sink + shifted)
    return sizes[jax.random.permutation(jax.random.fold_in(own_key, 2), number_of)]


def normal_values(rng, shape, width, limit, pieces=(), kind=jnp.bfloat16):
    result = jax.random.normal(rng, shape, jnp.float32) * width
    if len(pieces) > 0:
        result = levels(rng, shape, pieces, -0.22, 0.18) * result
    return jnp.clip(result, min=-limit, max=limit).astype(kind)


def setup_inputs(seed: int = 0, part: int = 0) -> dict:
    key_of = jax.random.split(jax.random.key(seed), 9)
    part_keys = jax.random.split(jax.random.fold_in(key_of[8], part), 9)
    hidden_acts = normal_values(part_keys[0], (TOKENS, FFW), 1.0, 6.0, ((0, 4), (1, 4)))
    cotangent = normal_values(part_keys[1], (TOKENS, D), 0.1, 0.796875, ((0, 4), (1, 4)))
    lengths = ragged_sizes(part_keys[2], EXAMPLES, TOKENS, MOST, 2).astype(jnp.int32)
    row_signs = draw_row_signs(jax.random.fold_in(key_of[8], 71), part)
    col_signs = draw_col_signs(jax.random.fold_in(key_of[8], 71), part)
    feat_row = place_ends(jax.random.randint(key_of[5], (K,), 0, FFW), jax.random.fold_in(key_of[5], 1), 0, FFW - 1).astype(jnp.int32)
    feat_col = place_ends(jax.random.randint(key_of[6], (K,), 0, D), jax.random.fold_in(key_of[6], 1), 0, D - 1).astype(jnp.int32)
    inverse_rows = draw_inverse_rows(jax.random.fold_in(key_of[8], 71), part)
    return {"hidden_acts": hidden_acts, "cotangent": cotangent, "lengths": lengths, "row_signs": row_signs, "col_signs": col_signs, "feat_row": feat_row, "feat_col": feat_col, "inverse_rows": inverse_rows}


def hadamard(mat_size):
    indices = jnp.arange(mat_size, dtype=jnp.int32)
    common = indices[:, None] & indices[None, :]
    parity = jnp.zeros((mat_size, mat_size), jnp.int32)
    for bit_pos in range(max(mat_size.bit_length() - 1, 0)):
        parity = parity + (common >> bit_pos & 1)
    return (1 - 2 * (parity % 2)).astype(jnp.float32)

def kron_apply(values, outer_mat, inner_mat):
    tokens = values.shape[0]
    shaped = values.reshape(tokens, outer_mat.shape[0], inner_mat.shape[0])
    shaped = jnp.einsum('tri,ia->tra', shaped, inner_mat, precision=lax.Precision.HIGHEST)
    shaped = jnp.einsum('tra,rh->tha', shaped, outer_mat, precision=lax.Precision.HIGHEST)
    return shaped.reshape(tokens, -1)

def reference(hidden_acts, cotangent, lengths, row_signs, col_signs, feat_row, feat_col, inverse_rows):
    left_side = hidden_acts.astype(jnp.float32) * row_signs.astype(jnp.float32)[None, :]
    left_side = kron_apply(left_side, hadamard(N_ROWS), hadamard(FFW_DEV))
    inner_width = min(D, 128)
    right_side = cotangent.astype(jnp.float32) * col_signs.astype(jnp.float32)[None, :]
    right_side = kron_apply(right_side, hadamard(D // inner_width), hadamard(inner_width))
    ex_end = jnp.cumsum(lengths).astype(jnp.int32)
    positions = jnp.arange(TOKENS, dtype=jnp.int32)
    owner = lax.optimization_barrier(jnp.sum((positions[:, None] >= ex_end[None, :]).astype(jnp.int32), axis=1))
    member = (owner[:, None] == jnp.arange(EXAMPLES, dtype=jnp.int32)[None, :]).astype(jnp.float32)
    picked = jnp.take(left_side, feat_row, axis=1) * jnp.take(right_side, feat_col, axis=1)
    features = jnp.dot(member.T, picked, precision=lax.Precision.HIGHEST) * (1.0 / math.sqrt(FFW * D))
    features_low = features.astype(jnp.bfloat16)
    return jnp.dot(features_low, inverse_rows, preferred_element_type=jnp.float32).astype(jnp.bfloat16)
```

```python
import functools
import math

import jax
import jax.numpy as jnp
from jax import lax
from jax.experimental import pallas as pl
from jax.experimental.pallas import tpu as pltpu
from jax.sharding import PartitionSpec as P


def signs(first_bits, second_bits):
    odd = lax.population_count(first_bits & second_bits) & 1
    return (1 - 2 * odd).astype(jnp.float32).astype(jnp.bfloat16)


def sign_rows(first, count, step, picks):
    inner = lax.broadcasted_iota(jnp.int32, (step, picks.shape[1]), 0)
    table = signs(inner, picks)
    parts = [table * signs(jnp.zeros_like(picks) + (first + n * step), picks) for n in range(count)]
    return parts[0] if count == 1 else jnp.concatenate(parts, axis=0)


def loop(count, body):
    if count <= 4:
        for n in range(count):
            body(n)
    else:
        lax.fori_loop(0, count, lambda n, c: (body(n), c)[1], 0)


def when(cond, body):
    if isinstance(cond, bool):
        if cond:
            body()
    else:
        pl.when(cond)(body)


def kernel(
    row_count,
    ex_count,
    norm_scale,
    hid_ref,
    cot_ref,
    len_ref,
    rsign_ref,
    csign_ref,
    frow_ref,
    fcol_ref,
    inv_ref,
    out_ref,
    hid_all,
    cot_signed,
    right_buf,
    part_buf,
    ex_in,
    row_out,
    row_in,
    score_out,
    score_in,
    inv_buf,
    total_buf,
    inv_sem,
    hid_send,
    hid_recv,
    ex_send,
    ex_recv,
    row_send,
    row_recv,
    score_send,
    score_recv,
):
    row = lax.axis_index("rows")
    ex = lax.axis_index("ex")
    tok_dev, width = hid_ref.shape
    cot_width = cot_ref.shape[1]
    features = frow_ref.shape[1]
    own = features // row_count
    examples = len_ref.shape[1]
    chunk = min(own, 512)
    ex_steps = ex_count.bit_length() - 1

    def block_of(i):
        return lax.rem(row + 1 + i, row_count)

    def inv_copy(n):
        cols = pl.ds(pl.multiple_of(block_of(n) * own, 128), own)
        return pltpu.make_async_copy(inv_ref.at[:, cols], inv_buf.at[n], inv_sem.at[n])

    barrier = pltpu.get_barrier_semaphore()

    def greet(n):
        pl.semaphore_signal(
            barrier,
            inc=1,
            device_id={"rows": lax.rem(row + n + 1, row_count)},
            device_id_type=pl.DeviceIdType.MESH,
        )

    loop(row_count - 1, greet)

    def bit_of(step):
        return lax.rem(ex // (1 << step), 2)

    def partner_of(step):
        return ex + (1 - 2 * bit_of(step)) * (1 << step)

    for step in range(ex_steps):
        pl.semaphore_signal(
            barrier,
            inc=1,
            device_id={"ex": partner_of(step)},
            device_id_type=pl.DeviceIdType.MESH,
        )
    loop(row_count, lambda n: inv_copy(n).start())
    hid_all[row] = hid_ref[...] * rsign_ref[...].astype(jnp.float32).astype(jnp.bfloat16)
    if csign_ref.shape[1] == cot_width:
        col_sign = csign_ref[...]
    else:
        col_sign = csign_ref[:, pl.ds(pl.multiple_of(row * cot_width, 128), cot_width)]
    cot_signed[...] = cot_ref[...] * col_sign.astype(jnp.float32).astype(jnp.bfloat16)
    lens = jnp.broadcast_to(len_ref[...].astype(jnp.float32), (examples, examples))
    e_row = lax.broadcasted_iota(jnp.int32, (examples, examples), 0)
    e_col = lax.broadcasted_iota(jnp.int32, (examples, examples), 1)
    ends = jnp.sum(jnp.where(e_col <= e_row, lens, 0.0), axis=1, keepdims=True)
    starts = jnp.sum(jnp.where(e_col < e_row, lens, 0.0), axis=1, keepdims=True)
    spots = ex * tok_dev + lax.broadcasted_iota(jnp.int32, (examples, tok_dev), 1)
    spots = spots.astype(jnp.float32)
    member = jnp.where((spots >= starts) & (spots < ends), 1.0, 0.0).astype(jnp.bfloat16)
    pl.semaphore_wait(barrier, row_count - 1 + ex_steps)

    def hid_copy(n, incoming=False):
        to = lax.rem(row + n + 1, row_count)
        block = lax.rem(row - n - 1 + row_count, row_count) if incoming else row
        return pltpu.make_async_remote_copy(
            src_ref=hid_all.at[block],
            dst_ref=hid_all.at[block],
            send_sem=hid_send.at[n],
            recv_sem=hid_recv.at[n],
            device_id={"rows": to},
            device_id_type=pl.DeviceIdType.MESH,
        )

    loop(row_count - 1, lambda n: hid_copy(n).start())

    def picks_of(ref, i, c):
        at = pl.multiple_of(block_of(i) * own + c * chunk, 128)
        return ref[:, pl.ds(at, chunk)]

    inner = min(cot_width, 128)

    def right_side(i):
        def one(c):
            table = sign_rows(row * cot_width, cot_width // inner, inner, picks_of(fcol_ref, i, c))
            at = c * chunk if isinstance(c, int) else pl.multiple_of(c * chunk, 128)
            right_buf[i, :, pl.ds(at, chunk)] = jnp.dot(
                cot_signed[...], table, preferred_element_type=jnp.float32
            )

        loop(own // chunk, one)

    group = min(row_count, 4)

    def features_of(i):
        def one(c):
            picks = picks_of(frow_ref, i, c)

            def some(g, left):
                acts = jnp.concatenate([hid_all[g * group + n] for n in range(group)], axis=1)
                table = sign_rows(g * group * width, group, width, picks)
                return left + jnp.dot(acts, table, preferred_element_type=jnp.float32)

            left = jnp.zeros((tok_dev, chunk), jnp.float32)
            if row_count == group:
                left = some(0, left)
            else:
                left = lax.fori_loop(0, row_count // group, some, left)
            at = c * chunk if isinstance(c, int) else pl.multiple_of(c * chunk, 128)
            products = left * right_buf[i, :, pl.ds(at, chunk)]
            high = products.astype(jnp.bfloat16)
            rest = (products - high.astype(jnp.float32)).astype(jnp.bfloat16)
            sums = jnp.dot(member, high, preferred_element_type=jnp.float32)
            sums = sums + jnp.dot(member, rest, preferred_element_type=jnp.float32)
            part_buf[i, :, :, pl.ds(at, chunk)] = sums.reshape(ex_count, examples // ex_count, chunk)

        loop(own // chunk, one)

    def ex_copies(i, step):
        size = 1 << step
        first = ex_count - (ex_count >> step)
        copies = []
        for m in range(ex_count >> (step + 1)):
            away = lax.rem(ex, size) + (1 - bit_of(step)) * size + m * 2 * size
            slot = first + m
            copies.append(
                pltpu.make_async_remote_copy(
                    src_ref=part_buf.at[i, away],
                    dst_ref=ex_in.at[i, slot],
                    send_sem=ex_send.at[i, slot],
                    recv_sem=ex_recv.at[i, slot],
                    device_id={"ex": partner_of(step)},
                    device_id_type=pl.DeviceIdType.MESH,
                )
            )
        return copies

    def ex_start(i, step):
        for copy in ex_copies(i, step):
            copy.start()

    def ex_finish(i, step):
        size = 1 << step
        first = ex_count - (ex_count >> step)
        for m, copy in enumerate(ex_copies(i, step)):
            copy.wait_recv()
            mine = lax.rem(ex, 2 * size) + m * 2 * size
            part_buf[i, mine] = part_buf[i, mine] + ex_in[i, first + m]

    def row_copy(i):
        return pltpu.make_async_remote_copy(
            src_ref=row_out.at[i],
            dst_ref=row_in.at[i],
            send_sem=row_send.at[i],
            recv_sem=row_recv.at[i],
            device_id={"rows": block_of(i)},
            device_id_type=pl.DeviceIdType.MESH,
        )

    def stage(i, step):
        def work():
            if step > 0:
                ex_finish(i, step - 1)
            if step < ex_steps:
                ex_start(i, step)
            else:


                def send():
                    row_out[i] = part_buf[i, ex].astype(row_out.dtype)
                    row_copy(i).start()

                when(i < row_count - 1, send)

        return work

    loop(row_count, right_side)
    loop(row_count - 1, lambda n: hid_copy(n, True).wait_recv())

    def block_step(i):
        features_of(i)
        stage(i, 0)()
        for step in range(1, ex_steps + 1):
            when(i >= step, stage(i - step, step))

    loop(row_count, block_step)
    for late in range(1, ex_steps + 1):
        for step in range(late, ex_steps + 1):
            if row_count - 1 + late - step >= 0:
                stage(row_count - 1 + late - step, step)()

    total_buf[...] = part_buf[row_count - 1, ex]

    def add_row(n):
        row_copy(n).wait_recv()
        total_buf[...] = total_buf[...] + row_in[n].astype(jnp.float32)

    loop(row_count - 1, add_row)
    low = (total_buf[...] * norm_scale).astype(jnp.bfloat16)

    def score_copy(n):
        return pltpu.make_async_remote_copy(
            src_ref=score_out.at[n],
            dst_ref=score_in.at[n],
            send_sem=score_send.at[n],
            recv_sem=score_recv.at[n],
            device_id={"rows": block_of(n)},
            device_id_type=pl.DeviceIdType.MESH,
        )

    tile = min(own, 512)

    def score_block(n):
        inv_copy(n).wait()

        def one(j):
            at = j * tile if isinstance(j, int) else pl.multiple_of(j * tile, 128)
            got = jnp.dot(low, inv_buf[n, :, pl.ds(at, tile)], preferred_element_type=jnp.float32)

            def keep():
                total_buf[:, pl.ds(at, tile)] = got

            def give():
                score_out[n, :, pl.ds(at, tile)] = got.astype(score_out.dtype)

            when(n == row_count - 1, keep)
            when(n < row_count - 1, give)

        loop(own // tile, one)
        when(n < row_count - 1, lambda: score_copy(n).start())

    loop(row_count, score_block)
    def add_score(n):
        score_copy(n).wait_recv()
        total_buf[...] = total_buf[...] + score_in[n].astype(jnp.float32)

    loop(row_count - 1, add_score)
    out_ref[...] = total_buf[...].astype(out_ref.dtype)
    loop(row_count - 1, lambda n: hid_copy(n).wait_send())
    loop(row_count - 1, lambda n: score_copy(n).wait_send())
    loop(row_count - 1, lambda n: row_copy(n).wait_send())

    def ex_sent(i):
        for step in range(ex_steps):
            for copy in ex_copies(i, step):
                copy.wait_send()

    loop(row_count, ex_sent)


def pair_kernel(
    row_count,
    ex_count,
    norm_scale,
    hid_hbm,
    cot_hbm,
    len_hbm,
    rsign_hbm,
    csign_hbm,
    frow_hbm,
    fcol_hbm,
    inv_ref,
    out_ref,
    hid_buf,
    cot_buf,
    len_buf,
    rsign_buf,
    csign_buf,
    frow_buf,
    fcol_buf,
    hid_all,
    cot_all,
    right_table,
    left_table,
    right_buf,
    high_buf,
    rest_buf,
    part_buf,
    ex_out,
    ex_in,
    row_out,
    row_in,
    keep_buf,
    mate_buf,
    score_out,
    score_in,
    inv_buf,
    load_sem,
    inv_sem,
    hid_send,
    hid_recv,
    relay_send,
    relay_recv,
    cot_send,
    cot_recv,
    ex_send,
    ex_recv,
    row_send,
    row_recv,
    mate_send,
    mate_recv,
    score_send,
    score_recv,
):
    row = lax.axis_index("rows")
    ex = lax.axis_index("ex")
    core = lax.rem(ex, 2)
    mate = ex + 1 - 2 * core
    group = ex // 2
    groups = ex_count // 2
    tok_dev, width = hid_hbm.shape
    cot_width = cot_hbm.shape[1]
    features = frow_hbm.shape[1]
    own = features // row_count
    half = own // 2
    examples = len_hbm.shape[1]
    chunk = min(half, 512)
    mesh_id = pl.DeviceIdType.MESH
    last = row_count - 1

    def other_row(n):
        far, at = last - n, row
        for bit in range(row_count.bit_length() - 1):
            if far >> bit & 1:
                at = at + (1 - 2 * lax.rem(row // (1 << bit), 2)) * (1 << bit)
        return at

    def other_group(n):
        return lax.rem(group + 1 + n, groups)

    barrier = pltpu.get_barrier_semaphore()
    for n in range(last):
        pl.semaphore_signal(barrier, inc=1, device_id={"rows": other_row(n)}, device_id_type=mesh_id)
    for n in range(groups - 1):
        pl.semaphore_signal(
            barrier, inc=1, device_id={"ex": 2 * other_group(n) + core}, device_id_type=mesh_id
        )
    pl.semaphore_signal(barrier, inc=1, device_id={"ex": mate}, device_id_type=mesh_id)

    cols = pl.ds(pl.multiple_of(row * cot_width, 128), cot_width)
    loads = {
        name: pltpu.make_async_copy(source, target, load_sem.at[n])
        for n, (name, source, target) in enumerate(
            (
                ("hid", hid_hbm, hid_buf),
                ("rsign", rsign_hbm, rsign_buf),
                ("cot", cot_hbm, cot_buf),
                ("csign", csign_hbm.at[:, cols], csign_buf),
                ("fcol", fcol_hbm, fcol_buf),
                ("frow", frow_hbm, frow_buf),
                ("len", len_hbm, len_buf),
            )
        )
    }
    for load in loads.values():
        load.start()

    def inv_copy(n):
        target = pl.ds(pl.multiple_of(other_row(n) * own, 128), own)
        source = pl.ds(pl.multiple_of(core * half, 16), half)
        return pltpu.make_async_copy(inv_ref.at[source, target], inv_buf.at[n], inv_sem.at[n])

    def picks_of(ref, i, c):
        at = pl.multiple_of(other_row(i) * own + core * half + c * chunk, 128)
        return ref[:, pl.ds(at, chunk)]

    def spot(i, c):
        return slice(i * half + c * chunk, i * half + (c + 1) * chunk)

    inner = min(cot_width, 128)

    loads["hid"].wait()
    loads["rsign"].wait()
    hid_all[core, row] = hid_buf[...] * rsign_buf[...].astype(jnp.float32).astype(jnp.bfloat16)
    loads["cot"].wait()
    loads["csign"].wait()
    cot_all[core] = cot_buf[...] * csign_buf[...].astype(jnp.float32).astype(jnp.bfloat16)
    loads["fcol"].wait()

    def right_first(i):
        for c in range(half // chunk):
            table = sign_rows(row * cot_width, cot_width // inner, inner, picks_of(fcol_buf, i, c))
            right_table[:, spot(i, c)] = table
            right_buf[core, :, spot(i, c)] = jnp.dot(
                cot_all[core], table, preferred_element_type=jnp.float32
            )

    def right_mate(i):
        for c in range(half // chunk):
            right_buf[1 - core, :, spot(i, c)] = jnp.dot(
                cot_all[1 - core], right_table[:, spot(i, c)], preferred_element_type=jnp.float32
            )

    def hid_copy(n, block):
        return pltpu.make_async_remote_copy(
            src_ref=hid_all.at[core, block],
            dst_ref=hid_all.at[core, block],
            send_sem=hid_send.at[n],
            recv_sem=hid_recv.at[n],
            device_id={"rows": other_row(n)},
            device_id_type=mesh_id,
        )

    def relay_copy(n, side):
        return pltpu.make_async_remote_copy(
            src_ref=hid_all.at[side, other_row(n)],
            dst_ref=hid_all.at[side, other_row(n)],
            send_sem=relay_send.at[n],
            recv_sem=relay_recv.at[n],
            device_id={"ex": mate},
            device_id_type=mesh_id,
        )

    def cot_copy(side):
        return pltpu.make_async_remote_copy(
            src_ref=cot_all.at[side],
            dst_ref=cot_all.at[side],
            send_sem=cot_send,
            recv_sem=cot_recv,
            device_id={"ex": mate},
            device_id_type=mesh_id,
        )

    early = row_count // 2
    for i in range(early):
        right_first(i)
    pl.semaphore_wait(barrier, last + groups)
    for n in range(last):
        hid_copy(n, row).start()
    relay_copy(last, core).start()
    cot_copy(core).start()

    loads["len"].wait()
    lens = jnp.broadcast_to(len_buf[...].astype(jnp.float32), (examples, examples))
    e_row = lax.broadcasted_iota(jnp.int32, (examples, examples), 0)
    e_col = lax.broadcasted_iota(jnp.int32, (examples, examples), 1)
    ends = jnp.sum(jnp.where(e_col <= e_row, lens, 0.0), axis=1, keepdims=True)
    starts = jnp.sum(jnp.where(e_col < e_row, lens, 0.0), axis=1, keepdims=True)

    spots = 2 * group * tok_dev + lax.broadcasted_iota(jnp.int32, (examples, 2 * tok_dev), 1)
    spots = spots.astype(jnp.float32)
    member = jnp.where((spots >= starts) & (spots < ends), 1.0, 0.0).astype(jnp.bfloat16)

    for i in range(early, row_count):
        right_first(i)
    loads["frow"].wait()
    for i in range(row_count):
        for c in range(half // chunk):
            left_table[:, spot(i, c)] = sign_rows(0, row_count, width, picks_of(frow_buf, i, c))

    cot_copy(1 - core).wait_recv()
    for i in range(row_count):
        right_mate(i)

    for n in range(last):
        hid_copy(n, other_row(n)).wait_recv()
        relay_copy(n, core).start()
    for n in range(row_count):
        inv_copy(n).start()

    def products_of(side, tokens):
        acts = jnp.concatenate([hid_all[side, n] for n in range(row_count)], axis=1)
        for i in range(row_count):
            for c in range(half // chunk):
                left = jnp.dot(acts, left_table[:, spot(i, c)], preferred_element_type=jnp.float32)
                products = left * right_buf[side, :, spot(i, c)]
                high = products.astype(jnp.bfloat16)
                high_buf[tokens, spot(i, c)] = high
                rest_buf[tokens, spot(i, c)] = (products - high.astype(jnp.float32)).astype(jnp.bfloat16)

    own_tokens = pl.ds(pl.multiple_of(core * tok_dev, 16), tok_dev)
    mate_tokens = pl.ds(pl.multiple_of((1 - core) * tok_dev, 16), tok_dev)
    products_of(core, own_tokens)
    for n in range(row_count):
        relay_copy(n, 1 - core).wait_recv()
    products_of(1 - core, mate_tokens)

    def ex_copy(i, n):
        return pltpu.make_async_remote_copy(
            src_ref=ex_out.at[i, n],
            dst_ref=ex_in.at[i, n],
            send_sem=ex_send.at[i, n],
            recv_sem=ex_recv.at[i, n],
            device_id={"ex": 2 * other_group(n) + core},
            device_id_type=mesh_id,
        )

    def row_copy(i):
        return pltpu.make_async_remote_copy(
            src_ref=row_out.at[i],
            dst_ref=row_in.at[i],
            send_sem=row_send.at[i],
            recv_sem=row_recv.at[i],
            device_id={"rows": other_row(i)},
            device_id_type=mesh_id,
        )

    def sums_of(i):
        at = slice(i * half, (i + 1) * half)
        sums = jnp.dot(member, high_buf[:, at], preferred_element_type=jnp.float32)
        return sums + jnp.dot(member, rest_buf[:, at], preferred_element_type=jnp.float32)

    def ex_start(i, sums):
        part_buf[i] = sums.reshape(groups, examples // groups, half)
        for n in range(groups - 1):
            ex_out[i, n] = part_buf[i, other_group(n)].astype(ex_out.dtype)
            ex_copy(i, n).start()

    ready = sums_of(0)
    for i in range(1, row_count):
        later = sums_of(i)
        ex_start(i - 1, ready)
        ready = later
    ex_start(last, ready)

    total = None
    for i in range(row_count):
        total = part_buf[i, group]
        for n in range(groups - 1):
            ex_copy(i, n).wait_recv()
            total = total + ex_in[i, n].astype(jnp.float32)
        if i < last:
            row_out[i] = total.astype(row_out.dtype)
            row_copy(i).start()
    for n in range(last):
        row_copy(n).wait_recv()
        total = total + row_in[n].astype(jnp.float32)
    low = (total * norm_scale).astype(jnp.bfloat16)

    def mate_copy(n):
        return pltpu.make_async_remote_copy(
            src_ref=keep_buf.at[n, 1 - core],
            dst_ref=mate_buf.at[n],
            send_sem=mate_send.at[n],
            recv_sem=mate_recv.at[n],
            device_id={"ex": mate},
            device_id_type=mesh_id,
        )

    def score_copy(n):
        return pltpu.make_async_remote_copy(
            src_ref=score_out.at[n],
            dst_ref=score_in.at[n],
            send_sem=score_send.at[n],
            recv_sem=score_recv.at[n],
            device_id={"rows": other_row(n)},
            device_id_type=mesh_id,
        )

    tile = min(own, 512)
    owned = examples // ex_count

    def score_block(n):
        inv_copy(n).wait()
        for j in range(own // tile):
            at = slice(j * tile, (j + 1) * tile)
            got = jnp.dot(low, inv_buf[n, :, at], preferred_element_type=jnp.float32)
            keep_buf[n, :, :, at] = got.reshape(2, owned, tile)
        mate_copy(n).start()

    def score_sum(n):
        mate_copy(n).wait_recv()
        return keep_buf[n, core] + mate_buf[n]

    for n in range(row_count):
        score_block(n)
        if n >= 1:
            score_out[n - 1] = score_sum(n - 1).astype(score_out.dtype)
            score_copy(n - 1).start()
    total = score_sum(last)
    for n in range(last):
        score_copy(n).wait_recv()
        total = total + score_in[n].astype(jnp.float32)
    out_ref[...] = total.astype(out_ref.dtype)

    cot_copy(core).wait_send()
    for n in range(row_count):
        relay_copy(n, core).wait_send()
        mate_copy(n).wait_send()
        for m in range(groups - 1):
            ex_copy(n, m).wait_send()
    for n in range(last):
        hid_copy(n, row).wait_send()
        row_copy(n).wait_send()
        score_copy(n).wait_send()


def pair_call(row_count, ex_count, norm_scale, operands):
    hidden_acts, cotangent, lengths, frow = operands[0], operands[1], operands[2], operands[5]
    tok_dev, width = hidden_acts.shape
    cot_width = cotangent.shape[1]
    examples = lengths.shape[1]
    features = frow.shape[1]
    own = features // row_count
    half = own // 2
    groups = ex_count // 2
    owned = examples // ex_count
    last, others = row_count - 1, max(groups - 1, 1)
    dma = pltpu.SemaphoreType.DMA
    low, wide, whole = jnp.bfloat16, jnp.float32, jnp.int32
    vmem = pltpu.VMEM
    return pl.pallas_call(
        functools.partial(pair_kernel, row_count, ex_count, norm_scale),
        out_shape=jax.ShapeDtypeStruct((owned, own), low),
        in_specs=[pl.BlockSpec(memory_space=pltpu.HBM)] * 8,
        out_specs=pl.BlockSpec(memory_space=pltpu.VMEM),
        scratch_shapes=[
            vmem((tok_dev, width), low),
            vmem((tok_dev, cot_width), low),
            vmem((1, examples), whole),
            vmem((1, width), whole),
            vmem((1, cot_width), whole),
            vmem((1, features), whole),
            vmem((1, features), whole),
            vmem((2, row_count, tok_dev, width), low),
            vmem((2, tok_dev, cot_width), low),
            vmem((cot_width, row_count * half), low),
            vmem((row_count * width, row_count * half), low),
            vmem((2, tok_dev, row_count * half), wide),
            vmem((2 * tok_dev, row_count * half), low),
            vmem((2 * tok_dev, row_count * half), low),
            vmem((row_count, groups, examples // groups, half), wide),
            vmem((row_count, others, examples // groups, half), low),
            vmem((row_count, others, examples // groups, half), low),
            vmem((last, examples // groups, half), low),
            vmem((last, examples // groups, half), low),
            vmem((row_count, 2, owned, own), wide),
            vmem((row_count, owned, own), wide),
            vmem((last, owned, own), low),
            vmem((last, owned, own), low),
            vmem((row_count, half, own), low),
            dma((7,)),
            dma((row_count,)),
            dma((last,)),
            dma((last,)),
            dma((row_count,)),
            dma((row_count,)),
            dma,
            dma,
            dma((row_count, others)),
            dma((row_count, others)),
            dma((last,)),
            dma((last,)),
            dma((row_count,)),
            dma((row_count,)),
            dma((last,)),
            dma((last,)),
        ],
        compiler_params=pltpu.CompilerParams(
            collective_id=0, has_side_effects=True, vmem_limit_bytes=48 * 1024 * 1024
        ),
        name="features_and_scores",
    )(*[pltpu.with_memory_space_constraint(operand, pltpu.HBM) for operand in operands])


def local(hidden_acts, cotangent, lengths, row_signs, col_signs, feat_row, feat_col, inverse_rows):
    row_count = lax.axis_size("rows")
    ex_count = lax.axis_size("ex")
    tok_dev, width = hidden_acts.shape
    cot_width = cotangent.shape[1]
    features = feat_row.shape[0]
    examples = lengths.shape[0]
    own = features // row_count
    owned = examples // ex_count
    norm_scale = 1.0 / math.sqrt(width * row_count * col_signs.shape[0])
    operands = (
        hidden_acts,
        cotangent,
        lengths.reshape(1, -1),
        row_signs.reshape(1, -1),
        col_signs.reshape(1, -1),
        feat_row.reshape(1, -1),
        feat_col.reshape(1, -1),
        inverse_rows,
    )
    if (
        ex_count % 2 == 0
        and row_count in (2, 4, 8)
        and own % 256 == 0
        and cot_width % 128 == 0
        and width % 128 == 0
        and tok_dev % 16 == 0
        and owned % 8 == 0
        and features * (width * row_count + cot_width + own) <= 32 * 1024 * 1024
    ):
        return pair_call(row_count, ex_count, norm_scale, operands)
    if cot_width % 128 != 0:
        col_signs = lax.dynamic_slice(col_signs, (lax.axis_index("rows") * cot_width,), (cot_width,))
    vmem = pl.BlockSpec(memory_space=pltpu.VMEM)
    others = max(row_count - 1, 1)
    dma = pltpu.SemaphoreType.DMA
    return pl.pallas_call(
        functools.partial(kernel, row_count, ex_count, norm_scale),
        out_shape=jax.ShapeDtypeStruct((owned, own), jnp.bfloat16),
        in_specs=[vmem] * 7 + [pl.BlockSpec(memory_space=pl.ANY)],
        out_specs=vmem,
        scratch_shapes=[
            pltpu.VMEM((row_count, tok_dev, width), jnp.bfloat16),
            pltpu.VMEM((tok_dev, cot_width), jnp.bfloat16),
            pltpu.VMEM((row_count, tok_dev, own), jnp.float32),
            pltpu.VMEM((row_count, ex_count, owned, own), jnp.float32),
            pltpu.VMEM((row_count, max(ex_count - 1, 1), owned, own), jnp.float32),
            pltpu.VMEM((others, owned, own), jnp.bfloat16),
            pltpu.VMEM((others, owned, own), jnp.bfloat16),
            pltpu.VMEM((others, owned, own), jnp.bfloat16),
            pltpu.VMEM((others, owned, own), jnp.bfloat16),
            pltpu.VMEM((row_count, own, own), jnp.bfloat16),
            pltpu.VMEM((owned, own), jnp.float32),
            dma((row_count,)),
            dma((others,)),
            dma((others,)),
            dma((row_count, max(ex_count - 1, 1))),
            dma((row_count, max(ex_count - 1, 1))),
            dma((others,)),
            dma((others,)),
            dma((others,)),
            dma((others,)),
        ],
        compiler_params=pltpu.CompilerParams(
            collective_id=0, has_side_effects=True, vmem_limit_bytes=60 * 1024 * 1024
        ),
        name="features_and_scores",
    )(
        hidden_acts,
        cotangent,
        lengths.reshape(1, -1),
        row_signs.reshape(1, -1),
        col_signs.reshape(1, -1),
        feat_row.reshape(1, -1),
        feat_col.reshape(1, -1),
        inverse_rows,
    )


def solution(mesh):
    placed = (
        P(("parts", "ex"), "rows"),
        P(("parts", "ex"), "rows"),
        P("parts"),
        P("rows"),
        P(),
        P(),
        P(),
        P("rows", None),
    )
    return jax.shard_map(
        local, mesh=mesh, in_specs=placed, out_specs=P(("parts", "ex"), "rows"), check_vma=False
    )
```

```python
import functools
import math

import jax
import jax.numpy as jnp
from jax import lax
from jax.experimental import pallas as pl
from jax.experimental.pallas import tpu as pltpu
from jax.sharding import PartitionSpec as P


def signs(first_bits, second_bits):
    odd = lax.population_count(first_bits & second_bits) & 1
    return (1 - 2 * odd).astype(jnp.float32).astype(jnp.bfloat16)


def sign_rows(first, count, step, picks):
    inner = lax.broadcasted_iota(jnp.int32, (step, picks.shape[1]), 0)
    table = signs(inner, picks)
    parts = [table * signs(jnp.zeros_like(picks) + (first + n * step), picks) for n in range(count)]
    return parts[0] if count == 1 else jnp.concatenate(parts, axis=0)


def loop(count, body):
    if count <= 4:
        for n in range(count):
            body(n)
    else:
        lax.fori_loop(0, count, lambda n, c: (body(n), c)[1], 0)


def when(cond, body):
    if isinstance(cond, bool):
        if cond:
            body()
    else:
        pl.when(cond)(body)


def kernel(
    row_count,
    ex_count,
    norm_scale,
    hid_ref,
    cot_ref,
    len_ref,
    rsign_ref,
    csign_ref,
    frow_ref,
    fcol_ref,
    inv_ref,
    out_ref,
    hid_all,
    cot_signed,
    right_buf,
    part_buf,
    ex_in,
    row_out,
    row_in,
    score_out,
    score_in,
    inv_buf,
    total_buf,
    inv_sem,
    hid_send,
    hid_recv,
    ex_send,
    ex_recv,
    row_send,
    row_recv,
    score_send,
    score_recv,
):
    row = lax.axis_index("rows")
    ex = lax.axis_index("ex")
    tok_dev, width = hid_ref.shape
    cot_width = cot_ref.shape[1]
    features = frow_ref.shape[1]
    own = features // row_count
    examples = len_ref.shape[1]
    chunk = min(own, 512)
    ex_steps = ex_count.bit_length() - 1

    def block_of(i):
        return lax.rem(row + 1 + i, row_count)

    def inv_copy(n):
        cols = pl.ds(pl.multiple_of(block_of(n) * own, 128), own)
        return pltpu.make_async_copy(inv_ref.at[:, cols], inv_buf.at[n], inv_sem.at[n])

    barrier = pltpu.get_barrier_semaphore()

    def greet(n):
        pl.semaphore_signal(
            barrier,
            inc=1,
            device_id={"rows": lax.rem(row + n + 1, row_count)},
            device_id_type=pl.DeviceIdType.MESH,
        )

    loop(row_count - 1, greet)

    def bit_of(step):
        return lax.rem(ex // (1 << step), 2)

    def partner_of(step):
        return ex + (1 - 2 * bit_of(step)) * (1 << step)

    for step in range(ex_steps):
        pl.semaphore_signal(
            barrier,
            inc=1,
            device_id={"ex": partner_of(step)},
            device_id_type=pl.DeviceIdType.MESH,
        )
    loop(row_count, lambda n: inv_copy(n).start())
    hid_all[row] = hid_ref[...] * rsign_ref[...].astype(jnp.float32).astype(jnp.bfloat16)
    if csign_ref.shape[1] == cot_width:
        col_sign = csign_ref[...]
    else:
        col_sign = csign_ref[:, pl.ds(pl.multiple_of(row * cot_width, 128), cot_width)]
    cot_signed[...] = cot_ref[...] * col_sign.astype(jnp.float32).astype(jnp.bfloat16)
    lens = jnp.broadcast_to(len_ref[...].astype(jnp.float32), (examples, examples))
    e_row = lax.broadcasted_iota(jnp.int32, (examples, examples), 0)
    e_col = lax.broadcasted_iota(jnp.int32, (examples, examples), 1)
    ends = jnp.sum(jnp.where(e_col <= e_row, lens, 0.0), axis=1, keepdims=True)
    starts = jnp.sum(jnp.where(e_col < e_row, lens, 0.0), axis=1, keepdims=True)
    spots = ex * tok_dev + lax.broadcasted_iota(jnp.int32, (examples, tok_dev), 1)
    spots = spots.astype(jnp.float32)
    member = jnp.where((spots >= starts) & (spots < ends), 1.0, 0.0).astype(jnp.bfloat16)
    pl.semaphore_wait(barrier, row_count - 1 + ex_steps)

    def hid_copy(n, incoming=False):
        to = lax.rem(row + n + 1, row_count)
        block = lax.rem(row - n - 1 + row_count, row_count) if incoming else row
        return pltpu.make_async_remote_copy(
            src_ref=hid_all.at[block],
            dst_ref=hid_all.at[block],
            send_sem=hid_send.at[n],
            recv_sem=hid_recv.at[n],
            device_id={"rows": to},
            device_id_type=pl.DeviceIdType.MESH,
        )

    loop(row_count - 1, lambda n: hid_copy(n).start())

    def picks_of(ref, i, c):
        at = pl.multiple_of(block_of(i) * own + c * chunk, 128)
        return ref[:, pl.ds(at, chunk)]

    inner = min(cot_width, 128)

    def right_side(i):
        def one(c):
            table = sign_rows(row * cot_width, cot_width // inner, inner, picks_of(fcol_ref, i, c))
            at = c * chunk if isinstance(c, int) else pl.multiple_of(c * chunk, 128)
            right_buf[i, :, pl.ds(at, chunk)] = jnp.dot(
                cot_signed[...], table, preferred_element_type=jnp.float32
            )

        loop(own // chunk, one)

    group = min(row_count, 4)

    def features_of(i):
        def one(c):
            picks = picks_of(frow_ref, i, c)

            def some(g, left):
                acts = jnp.concatenate([hid_all[g * group + n] for n in range(group)], axis=1)
                table = sign_rows(g * group * width, group, width, picks)
                return left + jnp.dot(acts, table, preferred_element_type=jnp.float32)

            left = jnp.zeros((tok_dev, chunk), jnp.float32)
            if row_count == group:
                left = some(0, left)
            else:
                left = lax.fori_loop(0, row_count // group, some, left)
            at = c * chunk if isinstance(c, int) else pl.multiple_of(c * chunk, 128)
            products = left * right_buf[i, :, pl.ds(at, chunk)]
            high = products.astype(jnp.bfloat16)
            rest = (products - high.astype(jnp.float32)).astype(jnp.bfloat16)
            sums = jnp.dot(member, high, preferred_element_type=jnp.float32)
            sums = sums + jnp.dot(member, rest, preferred_element_type=jnp.float32)
            part_buf[i, :, :, pl.ds(at, chunk)] = sums.reshape(ex_count, examples // ex_count, chunk)

        loop(own // chunk, one)

    def ex_copies(i, step):
        size = 1 << step
        first = ex_count - (ex_count >> step)
        copies = []
        for m in range(ex_count >> (step + 1)):
            away = lax.rem(ex, size) + (1 - bit_of(step)) * size + m * 2 * size
            slot = first + m
            copies.append(
                pltpu.make_async_remote_copy(
                    src_ref=part_buf.at[i, away],
                    dst_ref=ex_in.at[i, slot],
                    send_sem=ex_send.at[i, slot],
                    recv_sem=ex_recv.at[i, slot],
                    device_id={"ex": partner_of(step)},
                    device_id_type=pl.DeviceIdType.MESH,
                )
            )
        return copies

    def ex_start(i, step):
        for copy in ex_copies(i, step):
            copy.start()

    def ex_finish(i, step):
        size = 1 << step
        first = ex_count - (ex_count >> step)
        for m, copy in enumerate(ex_copies(i, step)):
            copy.wait_recv()
            mine = lax.rem(ex, 2 * size) + m * 2 * size
            part_buf[i, mine] = part_buf[i, mine] + ex_in[i, first + m]

    def row_copy(i):
        return pltpu.make_async_remote_copy(
            src_ref=row_out.at[i],
            dst_ref=row_in.at[i],
            send_sem=row_send.at[i],
            recv_sem=row_recv.at[i],
            device_id={"rows": block_of(i)},
            device_id_type=pl.DeviceIdType.MESH,
        )

    def stage(i, step):
        def work():
            if step > 0:
                ex_finish(i, step - 1)
            if step < ex_steps:
                ex_start(i, step)
            else:


                def send():
                    row_out[i] = part_buf[i, ex].astype(row_out.dtype)
                    row_copy(i).start()

                when(i < row_count - 1, send)

        return work

    loop(row_count, right_side)
    loop(row_count - 1, lambda n: hid_copy(n, True).wait_recv())

    def block_step(i):
        features_of(i)
        stage(i, 0)()
        for step in range(1, ex_steps + 1):
            when(i >= step, stage(i - step, step))

    loop(row_count, block_step)
    for late in range(1, ex_steps + 1):
        for step in range(late, ex_steps + 1):
            if row_count - 1 + late - step >= 0:
                stage(row_count - 1 + late - step, step)()

    total_buf[...] = part_buf[row_count - 1, ex]

    def add_row(n):
        row_copy(n).wait_recv()
        total_buf[...] = total_buf[...] + row_in[n].astype(jnp.float32)

    loop(row_count - 1, add_row)
    low = (total_buf[...] * norm_scale).astype(jnp.bfloat16)

    def score_copy(n):
        return pltpu.make_async_remote_copy(
            src_ref=score_out.at[n],
            dst_ref=score_in.at[n],
            send_sem=score_send.at[n],
            recv_sem=score_recv.at[n],
            device_id={"rows": block_of(n)},
            device_id_type=pl.DeviceIdType.MESH,
        )

    tile = min(own, 512)

    def score_block(n):
        inv_copy(n).wait()

        def one(j):
            at = j * tile if isinstance(j, int) else pl.multiple_of(j * tile, 128)
            got = jnp.dot(low, inv_buf[n, :, pl.ds(at, tile)], preferred_element_type=jnp.float32)

            def keep():
                total_buf[:, pl.ds(at, tile)] = got

            def give():
                score_out[n, :, pl.ds(at, tile)] = got.astype(score_out.dtype)

            when(n == row_count - 1, keep)
            when(n < row_count - 1, give)

        loop(own // tile, one)
        when(n < row_count - 1, lambda: score_copy(n).start())

    loop(row_count, score_block)
    def add_score(n):
        score_copy(n).wait_recv()
        total_buf[...] = total_buf[...] + score_in[n].astype(jnp.float32)

    loop(row_count - 1, add_score)
    out_ref[...] = total_buf[...].astype(out_ref.dtype)
    loop(row_count - 1, lambda n: hid_copy(n).wait_send())
    loop(row_count - 1, lambda n: score_copy(n).wait_send())
    loop(row_count - 1, lambda n: row_copy(n).wait_send())

    def ex_sent(i):
        for step in range(ex_steps):
            for copy in ex_copies(i, step):
                copy.wait_send()

    loop(row_count, ex_sent)


def pair_kernel(
    row_count,
    ex_count,
    norm_scale,
    hid_hbm,
    cot_hbm,
    len_hbm,
    rsign_hbm,
    csign_hbm,
    frow_hbm,
    fcol_hbm,
    inv_ref,
    out_ref,
    hid_buf,
    cot_buf,
    len_buf,
    rsign_buf,
    csign_buf,
    frow_buf,
    fcol_buf,
    hid_all,
    cot_all,
    right_table,
    left_table,
    right_buf,
    high_buf,
    rest_buf,
    part_buf,
    ex_out,
    ex_in,
    row_out,
    row_in,
    keep_buf,
    mate_buf,
    score_out,
    score_in,
    inv_buf,
    load_sem,
    inv_sem,
    hid_send,
    hid_recv,
    relay_send,
    relay_recv,
    cot_send,
    cot_recv,
    ex_send,
    ex_recv,
    row_send,
    row_recv,
    mate_send,
    mate_recv,
    score_send,
    score_recv,
):
    row = lax.axis_index("rows")
    ex = lax.axis_index("ex")
    core = lax.rem(ex, 2)
    mate = ex + 1 - 2 * core
    group = ex // 2
    groups = ex_count // 2
    tok_dev, width = hid_hbm.shape
    cot_width = cot_hbm.shape[1]
    features = frow_hbm.shape[1]
    own = features // row_count
    half = own // 2
    examples = len_hbm.shape[1]
    chunk = min(half, 512)
    mesh_id = pl.DeviceIdType.MESH
    last = row_count - 1
    masks = sorted(range(row_count), key=lambda m: (m == 0, m != row_count // 2, -m))
    far = masks.index(last) if row_count == 4 else row_count
    by_distance = sorted(range(last), key=lambda n: -masks[n])

    def other_row(n):
        at = row
        for bit in range(row_count.bit_length() - 1):
            if masks[n] >> bit & 1:
                at = at + (1 - 2 * lax.rem(row // (1 << bit), 2)) * (1 << bit)
        return at

    def other_group(n):
        return lax.rem(group + 1 + n, groups)

    barrier = pltpu.get_barrier_semaphore()
    for n in range(last):
        pl.semaphore_signal(barrier, inc=1, device_id={"rows": other_row(n)}, device_id_type=mesh_id)
    for n in range(groups - 1):
        pl.semaphore_signal(
            barrier, inc=1, device_id={"ex": 2 * other_group(n) + core}, device_id_type=mesh_id
        )
    pl.semaphore_signal(barrier, inc=1, device_id={"ex": mate}, device_id_type=mesh_id)

    cols = pl.ds(pl.multiple_of(row * cot_width, 128), cot_width)
    loads = {
        name: pltpu.make_async_copy(source, target, load_sem.at[n])
        for n, (name, source, target) in enumerate(
            (
                ("hid", hid_hbm, hid_buf),
                ("rsign", rsign_hbm, rsign_buf),
                ("cot", cot_hbm, cot_buf),
                ("csign", csign_hbm.at[:, cols], csign_buf),
                ("fcol", fcol_hbm, fcol_buf),
                ("frow", frow_hbm, frow_buf),
                ("len", len_hbm, len_buf),
            )
        )
    }
    for load in loads.values():
        load.start()

    def score_row(n):
        return row if n == last else n + 1 - jnp.minimum(jnp.maximum(row - n, 0), 1)

    def inv_copy(n):
        target = pl.ds(pl.multiple_of(score_row(n) * own, 128), own)
        source = pl.ds(pl.multiple_of(core * half, 16), half)
        return pltpu.make_async_copy(inv_ref.at[source, target], inv_buf.at[n], inv_sem.at[n])

    def picks_of(ref, i, c):
        at = pl.multiple_of(other_row(i) * own + core * half + c * chunk, 128)
        return ref[:, pl.ds(at, chunk)]

    def spot(i, c):
        return slice(i * half + c * chunk, i * half + (c + 1) * chunk)

    inner = min(cot_width, 128)

    loads["hid"].wait()
    loads["rsign"].wait()
    hid_all[0, last] = hid_buf[...] * rsign_buf[...].astype(jnp.float32).astype(jnp.bfloat16)
    loads["cot"].wait()
    loads["csign"].wait()
    cot_all[0] = cot_buf[...] * csign_buf[...].astype(jnp.float32).astype(jnp.bfloat16)
    loads["fcol"].wait()

    def right_first(i):
        for c in range(half // chunk):
            table = sign_rows(row * cot_width, cot_width // inner, inner, picks_of(fcol_buf, i, c))
            right_table[:, spot(i, c)] = table
            right_buf[0, :, spot(i, c)] = jnp.dot(
                cot_all[0], table, preferred_element_type=jnp.float32
            )

    def right_mate(i):
        for c in range(half // chunk):
            right_buf[1, :, spot(i, c)] = jnp.dot(
                cot_all[1], right_table[:, spot(i, c)], preferred_element_type=jnp.float32
            )

    def hid_copy(n):
        return pltpu.make_async_remote_copy(
            src_ref=hid_all.at[0, last],
            dst_ref=hid_all.at[0, n],
            send_sem=hid_send.at[n],
            recv_sem=hid_recv.at[n],
            device_id={"rows": other_row(n)},
            device_id_type=mesh_id,
        )

    def relay_copy(n):
        return pltpu.make_async_remote_copy(
            src_ref=hid_all.at[0, n],
            dst_ref=hid_all.at[1, n],
            send_sem=relay_send.at[n],
            recv_sem=relay_recv.at[n],
            device_id={"ex": mate},
            device_id_type=mesh_id,
        )

    def cot_copy():
        return pltpu.make_async_remote_copy(
            src_ref=cot_all.at[0],
            dst_ref=cot_all.at[1],
            send_sem=cot_send,
            recv_sem=cot_recv,
            device_id={"ex": mate},
            device_id_type=mesh_id,
        )

    early = row_count // 2
    for i in range(early):
        right_first(i)
    pl.semaphore_wait(barrier, last + groups)
    for n in by_distance:
        hid_copy(n).start()
    relay_copy(last).start()
    cot_copy().start()

    loads["len"].wait()
    lens = jnp.broadcast_to(len_buf[...].astype(jnp.float32), (examples, examples))
    e_row = lax.broadcasted_iota(jnp.int32, (examples, examples), 0)
    e_col = lax.broadcasted_iota(jnp.int32, (examples, examples), 1)
    ends = jnp.sum(jnp.where(e_col <= e_row, lens, 0.0), axis=1, keepdims=True)
    starts = jnp.sum(jnp.where(e_col < e_row, lens, 0.0), axis=1, keepdims=True)

    spots = lax.broadcasted_iota(jnp.int32, (examples, 2 * tok_dev), 1)
    mates = (1 - 2 * core) * tok_dev
    spots = jnp.where(spots < tok_dev, spots, spots - tok_dev + mates) + ex * tok_dev
    spots = spots.astype(jnp.float32)
    member = jnp.where((spots >= starts) & (spots < ends), 1.0, 0.0).astype(jnp.bfloat16)

    for i in range(early, row_count):
        right_first(i)
    loads["frow"].wait()
    for i in range(row_count):
        for c in range(half // chunk):
            picks = picks_of(frow_buf, i, c)
            table = signs(lax.broadcasted_iota(jnp.int32, (width, chunk), 0), picks)
            for n in range(row_count):
                sign = signs(jnp.zeros_like(picks) + other_row(n) * width, picks)
                left_table[n * width : (n + 1) * width, spot(i, c)] = table * sign

    cot_copy().wait_recv()
    for i in range(row_count):
        right_mate(i)

    for n in range(last):
        hid_copy(n).wait_recv()
        relay_copy(n).start()
    for n in range(row_count):
        inv_copy(n).start()

    def acts_of(side):
        return jnp.concatenate([hid_all[side, n] for n in range(row_count)], axis=1)

    def products_of(side, i, acts):
        tokens = slice(side * tok_dev, (side + 1) * tok_dev)
        for c in range(half // chunk):
            left = jnp.dot(acts, left_table[:, spot(i, c)], preferred_element_type=jnp.float32)
            products = left * right_buf[side, :, spot(i, c)]
            high = products.astype(jnp.bfloat16)
            high_buf[tokens, spot(i, c)] = high
            rest_buf[tokens, spot(i, c)] = (products - high.astype(jnp.float32)).astype(jnp.bfloat16)

    def sums_of(i):
        at = slice(i * half, (i + 1) * half)
        sums = jnp.dot(member, high_buf[:, at], preferred_element_type=jnp.float32)
        sums = sums + jnp.dot(member, rest_buf[:, at], preferred_element_type=jnp.float32)
        part_buf[i] = sums.reshape(groups, examples // groups, half)

    def ex_copy(i, n):
        to = {"ex": 2 * other_group(n) + core}
        if i == far:
            to["rows"] = other_row(i)
        return pltpu.make_async_remote_copy(
            src_ref=ex_out.at[i, n],
            dst_ref=ex_in.at[i, n],
            send_sem=ex_send.at[i, n],
            recv_sem=ex_recv.at[i, n],
            device_id=to,
            device_id_type=mesh_id,
        )

    def row_copy(i):
        return pltpu.make_async_remote_copy(
            src_ref=row_out.at[i],
            dst_ref=row_in.at[i],
            send_sem=row_send.at[i],
            recv_sem=row_recv.at[i],
            device_id={"rows": other_row(i)},
            device_id_type=mesh_id,
        )

    def row_start(i, total):
        row_out[i] = total.astype(row_out.dtype)
        row_copy(i).start()

    def ex_start(i):
        for n in range(groups - 1):
            ex_out[i, n] = part_buf[i, other_group(n)].astype(ex_out.dtype)
            ex_copy(i, n).start()
        if i == far:
            row_start(i, part_buf[i, group])

    def ex_sum(i, total):
        for n in range(groups - 1):
            ex_copy(i, n).wait_recv()
            total = total + ex_in[i, n].astype(jnp.float32)
        return total

    acts = acts_of(0)
    for i in range(row_count):
        products_of(0, i, acts)
    for n in range(row_count):
        relay_copy(n).wait_recv()
    acts = acts_of(1)
    products_of(1, 0, acts)
    for i in range(row_count):
        if i < last:
            products_of(1, i + 1, acts)
        sums_of(i)
        ex_start(i)

    for i in range(last):
        if i != far:
            row_start(i, ex_sum(i, part_buf[i, group]))
    total = ex_sum(last, part_buf[last, group])
    for i in sorted(range(last), key=lambda i: masks[i]):
        row_copy(i).wait_recv()
        total = total + row_in[i].astype(jnp.float32)
        if i == far:
            total = ex_sum(i, total)
    low = (total * norm_scale).astype(jnp.bfloat16)

    def mate_copy(n):
        return pltpu.make_async_remote_copy(
            src_ref=keep_buf.at[n, 1 - core],
            dst_ref=mate_buf.at[n],
            send_sem=mate_send.at[n],
            recv_sem=mate_recv.at[n],
            device_id={"ex": mate},
            device_id_type=mesh_id,
        )

    def score_copy(n, slot):
        return pltpu.make_async_remote_copy(
            src_ref=score_out.at[n],
            dst_ref=score_in.at[slot],
            send_sem=score_send.at[n],
            recv_sem=score_recv.at[slot],
            device_id={"rows": score_row(n)},
            device_id_type=mesh_id,
        )

    tile = min(own, 512)
    owned = examples // ex_count

    def score_block(n):
        inv_copy(n).wait()
        for j in range(own // tile):
            at = slice(j * tile, (j + 1) * tile)
            got = jnp.dot(low, inv_buf[n, :, at], preferred_element_type=jnp.float32)
            keep_buf[n, :, :, at] = got.reshape(2, owned, tile)
        mate_copy(n).start()

    def score_sum(n):
        mate_copy(n).wait_recv()
        return keep_buf[n, core] + mate_buf[n]

    for n in range(row_count):
        score_block(n)
        if n >= 1:
            score_out[n - 1] = score_sum(n - 1).astype(score_out.dtype)
            score_copy(n - 1, row - 1 + jnp.minimum(jnp.maximum(score_row(n - 1) - row, 0), 1)).start()
    total = score_sum(last)
    for n in range(last):
        score_copy(n, n).wait_recv()
        total = total + score_in[n].astype(jnp.float32)
    out_ref[...] = total.astype(out_ref.dtype)

    cot_copy().wait_send()
    for n in range(row_count):
        relay_copy(n).wait_send()
        mate_copy(n).wait_send()
        for m in range(groups - 1):
            ex_copy(n, m).wait_send()
    for n in range(last):
        hid_copy(n).wait_send()
        row_copy(n).wait_send()
        score_copy(n, n).wait_send()


def pair_call(row_count, ex_count, norm_scale, operands):
    hidden_acts, cotangent, lengths, frow = operands[0], operands[1], operands[2], operands[5]
    tok_dev, width = hidden_acts.shape
    cot_width = cotangent.shape[1]
    examples = lengths.shape[1]
    features = frow.shape[1]
    own = features // row_count
    half = own // 2
    groups = ex_count // 2
    owned = examples // ex_count
    last, others = row_count - 1, max(groups - 1, 1)
    dma = pltpu.SemaphoreType.DMA
    low, wide, whole = jnp.bfloat16, jnp.float32, jnp.int32
    vmem = pltpu.VMEM
    return pl.pallas_call(
        functools.partial(pair_kernel, row_count, ex_count, norm_scale),
        out_shape=jax.ShapeDtypeStruct((owned, own), low),
        in_specs=[pl.BlockSpec(memory_space=pltpu.HBM)] * 8,
        out_specs=pl.BlockSpec(memory_space=pltpu.VMEM),
        scratch_shapes=[
            vmem((tok_dev, width), low),
            vmem((tok_dev, cot_width), low),
            vmem((1, examples), whole),
            vmem((1, width), whole),
            vmem((1, cot_width), whole),
            vmem((1, features), whole),
            vmem((1, features), whole),
            vmem((2, row_count, tok_dev, width), low),
            vmem((2, tok_dev, cot_width), low),
            vmem((cot_width, row_count * half), low),
            vmem((row_count * width, row_count * half), low),
            vmem((2, tok_dev, row_count * half), wide),
            vmem((2 * tok_dev, row_count * half), low),
            vmem((2 * tok_dev, row_count * half), low),
            vmem((row_count, groups, examples // groups, half), wide),
            vmem((row_count, others, examples // groups, half), low),
            vmem((row_count, others, examples // groups, half), low),
            vmem((last, examples // groups, half), low),
            vmem((last, examples // groups, half), low),
            vmem((row_count, 2, owned, own), wide),
            vmem((row_count, owned, own), wide),
            vmem((last, owned, own), low),
            vmem((last, owned, own), low),
            vmem((row_count, half, own), low),
            dma((7,)),
            dma((row_count,)),
            dma((last,)),
            dma((last,)),
            dma((row_count,)),
            dma((row_count,)),
            dma,
            dma,
            dma((row_count, others)),
            dma((row_count, others)),
            dma((last,)),
            dma((last,)),
            dma((row_count,)),
            dma((row_count,)),
            dma((last,)),
            dma((last,)),
        ],
        compiler_params=pltpu.CompilerParams(
            collective_id=0, has_side_effects=True, vmem_limit_bytes=48 * 1024 * 1024
        ),
        name="features_and_scores",
    )(*[pltpu.with_memory_space_constraint(operand, pltpu.HBM) for operand in operands])


def local(hidden_acts, cotangent, lengths, row_signs, col_signs, feat_row, feat_col, inverse_rows):
    row_count = lax.axis_size("rows")
    ex_count = lax.axis_size("ex")
    tok_dev, width = hidden_acts.shape
    cot_width = cotangent.shape[1]
    features = feat_row.shape[0]
    examples = lengths.shape[0]
    own = features // row_count
    owned = examples // ex_count
    norm_scale = 1.0 / math.sqrt(width * row_count * col_signs.shape[0])
    operands = (
        hidden_acts,
        cotangent,
        lengths.reshape(1, -1),
        row_signs.reshape(1, -1),
        col_signs.reshape(1, -1),
        feat_row.reshape(1, -1),
        feat_col.reshape(1, -1),
        inverse_rows,
    )
    if (
        ex_count % 2 == 0
        and row_count in (2, 4, 8)
        and own % 256 == 0
        and cot_width % 128 == 0
        and width % 128 == 0
        and tok_dev % 16 == 0
        and owned % 8 == 0
        and features * (width * row_count + cot_width + own) <= 32 * 1024 * 1024
    ):
        return pair_call(row_count, ex_count, norm_scale, operands)
    if cot_width % 128 != 0:
        col_signs = lax.dynamic_slice(col_signs, (lax.axis_index("rows") * cot_width,), (cot_width,))
    vmem = pl.BlockSpec(memory_space=pltpu.VMEM)
    others = max(row_count - 1, 1)
    dma = pltpu.SemaphoreType.DMA
    return pl.pallas_call(
        functools.partial(kernel, row_count, ex_count, norm_scale),
        out_shape=jax.ShapeDtypeStruct((owned, own), jnp.bfloat16),
        in_specs=[vmem] * 7 + [pl.BlockSpec(memory_space=pl.ANY)],
        out_specs=vmem,
        scratch_shapes=[
            pltpu.VMEM((row_count, tok_dev, width), jnp.bfloat16),
            pltpu.VMEM((tok_dev, cot_width), jnp.bfloat16),
            pltpu.VMEM((row_count, tok_dev, own), jnp.float32),
            pltpu.VMEM((row_count, ex_count, owned, own), jnp.float32),
            pltpu.VMEM((row_count, max(ex_count - 1, 1), owned, own), jnp.float32),
            pltpu.VMEM((others, owned, own), jnp.bfloat16),
            pltpu.VMEM((others, owned, own), jnp.bfloat16),
            pltpu.VMEM((others, owned, own), jnp.bfloat16),
            pltpu.VMEM((others, owned, own), jnp.bfloat16),
            pltpu.VMEM((row_count, own, own), jnp.bfloat16),
            pltpu.VMEM((owned, own), jnp.float32),
            dma((row_count,)),
            dma((others,)),
            dma((others,)),
            dma((row_count, max(ex_count - 1, 1))),
            dma((row_count, max(ex_count - 1, 1))),
            dma((others,)),
            dma((others,)),
            dma((others,)),
            dma((others,)),
        ],
        compiler_params=pltpu.CompilerParams(
            collective_id=0, has_side_effects=True, vmem_limit_bytes=60 * 1024 * 1024
        ),
        name="features_and_scores",
    )(
        hidden_acts,
        cotangent,
        lengths.reshape(1, -1),
        row_signs.reshape(1, -1),
        col_signs.reshape(1, -1),
        feat_row.reshape(1, -1),
        feat_col.reshape(1, -1),
        inverse_rows,
    )


def solution(mesh):
    placed = (
        P(("parts", "ex"), "rows"),
        P(("parts", "ex"), "rows"),
        P("parts"),
        P("rows"),
        P(),
        P(),
        P(),
        P("rows", None),
    )
    return jax.shard_map(
        local, mesh=mesh, in_specs=placed, out_specs=P(("parts", "ex"), "rows"), check_vma=False
    )
```

```python
import functools
import math

import jax
import jax.numpy as jnp
from jax import lax
from jax.experimental import pallas as pl
from jax.experimental.pallas import tpu as pltpu
from jax.sharding import PartitionSpec as P


def signs(first_bits, second_bits):
    odd = lax.population_count(first_bits & second_bits) & 1
    return (1 - 2 * odd).astype(jnp.float32).astype(jnp.bfloat16)


def sign_rows(first, count, step, picks):
    inner = lax.broadcasted_iota(jnp.int32, (step, picks.shape[1]), 0)
    table = signs(inner, picks)
    parts = [table * signs(jnp.zeros_like(picks) + (first + n * step), picks) for n in range(count)]
    return parts[0] if count == 1 else jnp.concatenate(parts, axis=0)


def loop(count, body):
    if count <= 4:
        for n in range(count):
            body(n)
    else:
        lax.fori_loop(0, count, lambda n, c: (body(n), c)[1], 0)


def when(cond, body):
    if isinstance(cond, bool):
        if cond:
            body()
    else:
        pl.when(cond)(body)


def kernel(
    row_count,
    ex_count,
    norm_scale,
    hid_ref,
    cot_ref,
    len_ref,
    rsign_ref,
    csign_ref,
    frow_ref,
    fcol_ref,
    inv_ref,
    out_ref,
    hid_all,
    cot_signed,
    right_buf,
    part_buf,
    ex_in,
    row_out,
    row_in,
    score_out,
    score_in,
    inv_buf,
    total_buf,
    inv_sem,
    hid_send,
    hid_recv,
    ex_send,
    ex_recv,
    row_send,
    row_recv,
    score_send,
    score_recv,
):
    row = lax.axis_index("rows")
    ex = lax.axis_index("ex")
    tok_dev, width = hid_ref.shape
    cot_width = cot_ref.shape[1]
    features = frow_ref.shape[1]
    own = features // row_count
    examples = len_ref.shape[1]
    chunk = min(own, 512)
    ex_steps = ex_count.bit_length() - 1

    def block_of(i):
        return lax.rem(row + 1 + i, row_count)

    def inv_copy(n):
        cols = pl.ds(pl.multiple_of(block_of(n) * own, 128), own)
        return pltpu.make_async_copy(inv_ref.at[:, cols], inv_buf.at[n], inv_sem.at[n])

    barrier = pltpu.get_barrier_semaphore()

    def greet(n):
        pl.semaphore_signal(
            barrier,
            inc=1,
            device_id={"rows": lax.rem(row + n + 1, row_count)},
            device_id_type=pl.DeviceIdType.MESH,
        )

    loop(row_count - 1, greet)

    def bit_of(step):
        return lax.rem(ex // (1 << step), 2)

    def partner_of(step):
        return ex + (1 - 2 * bit_of(step)) * (1 << step)

    for step in range(ex_steps):
        pl.semaphore_signal(
            barrier,
            inc=1,
            device_id={"ex": partner_of(step)},
            device_id_type=pl.DeviceIdType.MESH,
        )
    loop(row_count, lambda n: inv_copy(n).start())
    hid_all[row] = hid_ref[...] * rsign_ref[...].astype(jnp.float32).astype(jnp.bfloat16)
    if csign_ref.shape[1] == cot_width:
        col_sign = csign_ref[...]
    else:
        col_sign = csign_ref[:, pl.ds(pl.multiple_of(row * cot_width, 128), cot_width)]
    cot_signed[...] = cot_ref[...] * col_sign.astype(jnp.float32).astype(jnp.bfloat16)
    lens = jnp.broadcast_to(len_ref[...].astype(jnp.float32), (examples, examples))
    e_row = lax.broadcasted_iota(jnp.int32, (examples, examples), 0)
    e_col = lax.broadcasted_iota(jnp.int32, (examples, examples), 1)
    ends = jnp.sum(jnp.where(e_col <= e_row, lens, 0.0), axis=1, keepdims=True)
    starts = jnp.sum(jnp.where(e_col < e_row, lens, 0.0), axis=1, keepdims=True)
    spots = ex * tok_dev + lax.broadcasted_iota(jnp.int32, (examples, tok_dev), 1)
    spots = spots.astype(jnp.float32)
    member = jnp.where((spots >= starts) & (spots < ends), 1.0, 0.0).astype(jnp.bfloat16)
    pl.semaphore_wait(barrier, row_count - 1 + ex_steps)

    def hid_copy(n, incoming=False):
        to = lax.rem(row + n + 1, row_count)
        block = lax.rem(row - n - 1 + row_count, row_count) if incoming else row
        return pltpu.make_async_remote_copy(
            src_ref=hid_all.at[block],
            dst_ref=hid_all.at[block],
            send_sem=hid_send.at[n],
            recv_sem=hid_recv.at[n],
            device_id={"rows": to},
            device_id_type=pl.DeviceIdType.MESH,
        )

    loop(row_count - 1, lambda n: hid_copy(n).start())

    def picks_of(ref, i, c):
        at = pl.multiple_of(block_of(i) * own + c * chunk, 128)
        return ref[:, pl.ds(at, chunk)]

    inner = min(cot_width, 128)

    def right_side(i):
        def one(c):
            table = sign_rows(row * cot_width, cot_width // inner, inner, picks_of(fcol_ref, i, c))
            at = c * chunk if isinstance(c, int) else pl.multiple_of(c * chunk, 128)
            right_buf[i, :, pl.ds(at, chunk)] = jnp.dot(
                cot_signed[...], table, preferred_element_type=jnp.float32
            )

        loop(own // chunk, one)

    group = min(row_count, 4)

    def features_of(i):
        def one(c):
            picks = picks_of(frow_ref, i, c)

            def some(g, left):
                acts = jnp.concatenate([hid_all[g * group + n] for n in range(group)], axis=1)
                table = sign_rows(g * group * width, group, width, picks)
                return left + jnp.dot(acts, table, preferred_element_type=jnp.float32)

            left = jnp.zeros((tok_dev, chunk), jnp.float32)
            if row_count == group:
                left = some(0, left)
            else:
                left = lax.fori_loop(0, row_count // group, some, left)
            at = c * chunk if isinstance(c, int) else pl.multiple_of(c * chunk, 128)
            products = left * right_buf[i, :, pl.ds(at, chunk)]
            high = products.astype(jnp.bfloat16)
            rest = (products - high.astype(jnp.float32)).astype(jnp.bfloat16)
            sums = jnp.dot(member, high, preferred_element_type=jnp.float32)
            sums = sums + jnp.dot(member, rest, preferred_element_type=jnp.float32)
            part_buf[i, :, :, pl.ds(at, chunk)] = sums.reshape(ex_count, examples // ex_count, chunk)

        loop(own // chunk, one)

    def ex_copies(i, step):
        size = 1 << step
        first = ex_count - (ex_count >> step)
        copies = []
        for m in range(ex_count >> (step + 1)):
            away = lax.rem(ex, size) + (1 - bit_of(step)) * size + m * 2 * size
            slot = first + m
            copies.append(
                pltpu.make_async_remote_copy(
                    src_ref=part_buf.at[i, away],
                    dst_ref=ex_in.at[i, slot],
                    send_sem=ex_send.at[i, slot],
                    recv_sem=ex_recv.at[i, slot],
                    device_id={"ex": partner_of(step)},
                    device_id_type=pl.DeviceIdType.MESH,
                )
            )
        return copies

    def ex_start(i, step):
        for copy in ex_copies(i, step):
            copy.start()

    def ex_finish(i, step):
        size = 1 << step
        first = ex_count - (ex_count >> step)
        for m, copy in enumerate(ex_copies(i, step)):
            copy.wait_recv()
            mine = lax.rem(ex, 2 * size) + m * 2 * size
            part_buf[i, mine] = part_buf[i, mine] + ex_in[i, first + m]

    def row_copy(i):
        return pltpu.make_async_remote_copy(
            src_ref=row_out.at[i],
            dst_ref=row_in.at[i],
            send_sem=row_send.at[i],
            recv_sem=row_recv.at[i],
            device_id={"rows": block_of(i)},
            device_id_type=pl.DeviceIdType.MESH,
        )

    def stage(i, step):
        def work():
            if step > 0:
                ex_finish(i, step - 1)
            if step < ex_steps:
                ex_start(i, step)
            else:


                def send():
                    row_out[i] = part_buf[i, ex].astype(row_out.dtype)
                    row_copy(i).start()

                when(i < row_count - 1, send)

        return work

    loop(row_count, right_side)
    loop(row_count - 1, lambda n: hid_copy(n, True).wait_recv())

    def block_step(i):
        features_of(i)
        stage(i, 0)()
        for step in range(1, ex_steps + 1):
            when(i >= step, stage(i - step, step))

    loop(row_count, block_step)
    for late in range(1, ex_steps + 1):
        for step in range(late, ex_steps + 1):
            if row_count - 1 + late - step >= 0:
                stage(row_count - 1 + late - step, step)()

    total_buf[...] = part_buf[row_count - 1, ex]

    def add_row(n):
        row_copy(n).wait_recv()
        total_buf[...] = total_buf[...] + row_in[n].astype(jnp.float32)

    loop(row_count - 1, add_row)
    low = (total_buf[...] * norm_scale).astype(jnp.bfloat16)

    def score_copy(n):
        return pltpu.make_async_remote_copy(
            src_ref=score_out.at[n],
            dst_ref=score_in.at[n],
            send_sem=score_send.at[n],
            recv_sem=score_recv.at[n],
            device_id={"rows": block_of(n)},
            device_id_type=pl.DeviceIdType.MESH,
        )

    tile = min(own, 512)

    def score_block(n):
        inv_copy(n).wait()

        def one(j):
            at = j * tile if isinstance(j, int) else pl.multiple_of(j * tile, 128)
            got = jnp.dot(low, inv_buf[n, :, pl.ds(at, tile)], preferred_element_type=jnp.float32)

            def keep():
                total_buf[:, pl.ds(at, tile)] = got

            def give():
                score_out[n, :, pl.ds(at, tile)] = got.astype(score_out.dtype)

            when(n == row_count - 1, keep)
            when(n < row_count - 1, give)

        loop(own // tile, one)
        when(n < row_count - 1, lambda: score_copy(n).start())

    loop(row_count, score_block)
    def add_score(n):
        score_copy(n).wait_recv()
        total_buf[...] = total_buf[...] + score_in[n].astype(jnp.float32)

    loop(row_count - 1, add_score)
    out_ref[...] = total_buf[...].astype(out_ref.dtype)
    loop(row_count - 1, lambda n: hid_copy(n).wait_send())
    loop(row_count - 1, lambda n: score_copy(n).wait_send())
    loop(row_count - 1, lambda n: row_copy(n).wait_send())

    def ex_sent(i):
        for step in range(ex_steps):
            for copy in ex_copies(i, step):
                copy.wait_send()

    loop(row_count, ex_sent)


def pair_kernel(
    row_count,
    ex_count,
    norm_scale,
    hid_hbm,
    cot_hbm,
    len_hbm,
    rsign_hbm,
    csign_hbm,
    frow_hbm,
    fcol_hbm,
    inv_ref,
    out_ref,
    hid_buf,
    cot_buf,
    len_buf,
    rsign_buf,
    csign_buf,
    frow_buf,
    fcol_buf,
    hid_all,
    cot_all,
    left_table,
    right_buf,
    high_buf,
    rest_buf,
    part_buf,
    ex_out,
    ex_in,
    cross_in,
    total_buf,
    row_out,
    row_in,
    keep_buf,
    mate_buf,
    score_out,
    score_in,
    inv_buf,
    load_sem,
    inv_sem,
    hid_send,
    hid_recv,
    relay_send,
    relay_recv,
    cot_send,
    cot_recv,
    ex_send,
    ex_recv,
    cross_send,
    cross_recv,
    row_send,
    row_recv,
    mate_send,
    mate_recv,
    score_send,
    score_recv,
):
    row = lax.axis_index("rows")
    ex = lax.axis_index("ex")
    core = lax.rem(ex, 2)
    mate = ex + 1 - 2 * core
    group = ex // 2
    groups = ex_count // 2
    tok_dev, width = hid_hbm.shape
    cot_width = cot_hbm.shape[1]
    features = frow_hbm.shape[1]
    own = features // row_count
    half = own // 2
    examples = len_hbm.shape[1]
    chunk = min(half, 512)
    mesh_id = pl.DeviceIdType.MESH
    last = row_count - 1
    four = row_count == 4
    inside = lax.rem(row + 1, 4) // 2 if four else 1
    orders = ((3, 2, 1, 0), (2, 3, 1, 0)) if four else (tuple(range(last, -1, -1)),) * 2

    def pick(outer, inner):
        return outer + inside * (inner - outer)

    def flip(mask):
        at = row
        for bit in range(row_count.bit_length() - 1):
            if mask >> bit & 1:
                at = at + (1 - 2 * lax.rem(row // (1 << bit), 2)) * (1 << bit)
        return at

    def other_row(n):
        outer, inner = orders[0][n], orders[1][n]
        return flip(outer) if outer == inner else pick(flip(outer), flip(inner))

    def slot_there(n):
        if not four:
            return n
        return pick(orders[1 if orders[0][n] < last else 0].index(orders[0][n]), orders[0 if orders[1][n] < last else 1].index(orders[1][n]))

    def other_group(n):
        return lax.rem(group + 1 + n, groups)

    barrier = pltpu.get_barrier_semaphore()
    for n in range(last):
        pl.semaphore_signal(barrier, inc=1, device_id={"rows": other_row(n)}, device_id_type=mesh_id)
    for n in range(groups - 1):
        pl.semaphore_signal(
            barrier, inc=1, device_id={"ex": 2 * other_group(n) + core}, device_id_type=mesh_id
        )
    pl.semaphore_signal(barrier, inc=1, device_id={"ex": mate}, device_id_type=mesh_id)

    cols = pl.ds(pl.multiple_of(row * cot_width, 128), cot_width)
    loads = {
        name: pltpu.make_async_copy(source, target, load_sem.at[n])
        for n, (name, source, target) in enumerate(
            (
                ("hid", hid_hbm, hid_buf),
                ("rsign", rsign_hbm, rsign_buf),
                ("cot", cot_hbm, cot_buf),
                ("csign", csign_hbm.at[:, cols], csign_buf),
                ("fcol", fcol_hbm, fcol_buf),
                ("frow", frow_hbm, frow_buf),
                ("len", len_hbm, len_buf),
            )
        )
    }
    for load in loads.values():
        load.start()

    def score_row(n):
        return row if n == last else n + 1 - jnp.minimum(jnp.maximum(row - n, 0), 1)

    def inv_copy(n):
        target = pl.ds(pl.multiple_of(score_row(n) * own, 128), own)
        source = pl.ds(pl.multiple_of(core * half, 16), half)
        return pltpu.make_async_copy(inv_ref.at[source, target], inv_buf.at[n], inv_sem.at[n])

    def picks_of(ref, i, c):
        at = pl.multiple_of(other_row(i) * own + core * half + c * chunk, 128)
        return ref[:, pl.ds(at, chunk)]

    def spot(i, c):
        return slice(i * half + c * chunk, i * half + (c + 1) * chunk)

    loads["hid"].wait()
    loads["rsign"].wait()
    hid_all[0, last] = hid_buf[...] * rsign_buf[...].astype(jnp.float32).astype(jnp.bfloat16)
    loads["cot"].wait()
    loads["csign"].wait()
    cot_all[0] = cot_buf[...] * csign_buf[...].astype(jnp.float32).astype(jnp.bfloat16)
    loads["fcol"].wait()

    def short_rows(first, rows, picks):
        step = min(rows, 16)
        table = signs(lax.broadcasted_iota(jnp.int32, (step, chunk), 0), picks)
        table = table * signs(jnp.zeros_like(picks) + first, picks)
        blocks = signs(lax.broadcasted_iota(jnp.int32, (rows // step, chunk), 0) * step, picks)
        return jnp.concatenate([table * blocks[n : n + 1] for n in range(rows // step)], axis=0)

    def table_of(i, c):
        return short_rows(row * cot_width, cot_width, picks_of(fcol_buf, i, c))

    def right_first(i):
        for c in range(half // chunk):
            table = table_of(i, c)
            right_buf[0, :, spot(i, c)] = jnp.dot(
                cot_all[0], table, preferred_element_type=jnp.float32
            )

    def right_mate(i):
        for c in range(half // chunk):
            right_buf[1, :, spot(i, c)] = jnp.dot(
                cot_all[1], table_of(i, c), preferred_element_type=jnp.float32
            )

    def hid_copy(n, slot):
        return pltpu.make_async_remote_copy(
            src_ref=hid_all.at[0, last],
            dst_ref=hid_all.at[0, slot],
            send_sem=hid_send.at[n],
            recv_sem=hid_recv.at[slot],
            device_id={"rows": other_row(n)},
            device_id_type=mesh_id,
        )

    def relay_copy(n):
        return pltpu.make_async_remote_copy(
            src_ref=hid_all.at[0, n],
            dst_ref=hid_all.at[1, n],
            send_sem=relay_send.at[n],
            recv_sem=relay_recv.at[n],
            device_id={"ex": mate},
            device_id_type=mesh_id,
        )

    def cot_copy():
        return pltpu.make_async_remote_copy(
            src_ref=cot_all.at[0],
            dst_ref=cot_all.at[1],
            send_sem=cot_send,
            recv_sem=cot_recv,
            device_id={"ex": mate},
            device_id_type=mesh_id,
        )

    early = row_count // 2
    for i in range(early):
        right_first(i)
    pl.semaphore_wait(barrier, last + groups)
    for n in range(last):
        hid_copy(n, slot_there(n)).start()
    relay_copy(last).start()
    cot_copy().start()

    loads["len"].wait()
    lens = jnp.broadcast_to(len_buf[...].astype(jnp.float32), (examples, examples))
    e_row = lax.broadcasted_iota(jnp.int32, (examples, examples), 0)
    e_col = lax.broadcasted_iota(jnp.int32, (examples, examples), 1)
    ends = jnp.sum(jnp.where(e_col <= e_row, lens, 0.0), axis=1, keepdims=True)
    starts = jnp.sum(jnp.where(e_col < e_row, lens, 0.0), axis=1, keepdims=True)

    spots = lax.broadcasted_iota(jnp.int32, (examples, 2 * tok_dev), 1)
    mates = (1 - 2 * core) * tok_dev
    spots = jnp.where(spots < tok_dev, spots, spots - tok_dev + mates) + ex * tok_dev
    spots = spots.astype(jnp.float32)
    member = jnp.where((spots >= starts) & (spots < ends), 1.0, 0.0).astype(jnp.bfloat16)

    for i in range(early, row_count):
        right_first(i)
    loads["frow"].wait()
    for i in range(row_count):
        for c in range(half // chunk):
            picks = picks_of(frow_buf, i, c)
            for n in range(row_count):
                rows = slice(n * width, (n + 1) * width)
                left_table[rows, spot(i, c)] = short_rows(other_row(n) * width, width, picks)

    cot_copy().wait_recv()
    for i in range(row_count):
        right_mate(i)

    for n in range(last):
        hid_copy(n, n).wait_recv()
        relay_copy(n).start()
    for n in range(row_count):
        inv_copy(n).start()

    def acts_of(side):
        return jnp.concatenate([hid_all[side, n] for n in range(row_count)], axis=1)

    def products_of(side, i, acts):
        tokens = slice(side * tok_dev, (side + 1) * tok_dev)
        for c in range(half // chunk):
            left = jnp.dot(acts, left_table[:, spot(i, c)], preferred_element_type=jnp.float32)
            products = left * right_buf[side, :, spot(i, c)]
            high = products.astype(jnp.bfloat16)
            high_buf[tokens, spot(i, c)] = high
            rest_buf[tokens, spot(i, c)] = (products - high.astype(jnp.float32)).astype(jnp.bfloat16)

    def sums_of(i):
        at = slice(i * half, (i + 1) * half)
        sums = jnp.dot(member, high_buf[:, at], preferred_element_type=jnp.float32)
        sums = sums + jnp.dot(member, rest_buf[:, at], preferred_element_type=jnp.float32)
        part_buf[i] = sums.reshape(groups, examples // groups, half)

    def ex_copy(i, n):
        return pltpu.make_async_remote_copy(
            src_ref=ex_out.at[i, n],
            dst_ref=ex_in.at[i, n],
            send_sem=ex_send.at[i, n],
            recv_sem=ex_recv.at[i, n],
            device_id={"ex": 2 * other_group(n) + core},
            device_id_type=mesh_id,
        )

    def cross_copy(i, n, slot):
        return pltpu.make_async_remote_copy(
            src_ref=ex_out.at[i, n],
            dst_ref=cross_in.at[slot, n],
            send_sem=cross_send.at[i, n],
            recv_sem=cross_recv.at[slot, n],
            device_id={"rows": other_row(i), "ex": 2 * other_group(n) + core},
            device_id_type=mesh_id,
        )

    def when_inside(is_inside, body):
        if four:
            pl.when(inside == is_inside)(body)
        elif is_inside:
            body()

    def row_copy(i, slot):
        return pltpu.make_async_remote_copy(
            src_ref=row_out.at[i],
            dst_ref=row_in.at[slot],
            send_sem=row_send.at[i],
            recv_sem=row_recv.at[slot],
            device_id={"rows": other_row(i)},
            device_id_type=mesh_id,
        )

    def row_start(i, total):
        row_out[i] = total.astype(row_out.dtype)
        row_copy(i, slot_there(i)).start()

    def two_phase(i):
        for n in range(groups - 1):
            ex_copy(i, n).start()

    def one_phase(i):
        for n in range(groups - 1):
            cross_copy(i, n, slot_there(i)).start()
        row_start(i, part_buf[i, group])

    def ex_start(i):
        for n in range(groups - 1):
            ex_out[i, n] = part_buf[i, other_group(n)].astype(ex_out.dtype)
        if i == last:
            two_phase(i)
        else:
            when_inside(1, lambda: two_phase(i))
            when_inside(0, lambda: one_phase(i))

    def ex_sum(i, total):
        for n in range(groups - 1):
            ex_copy(i, n).wait_recv()
            total = total + ex_in[i, n].astype(jnp.float32)
        return total

    acts = acts_of(0)
    for i in range(row_count):
        products_of(0, i, acts)
    for n in range(row_count):
        relay_copy(n).wait_recv()
    acts = acts_of(1)
    for i in range(row_count):
        products_of(1, i, acts)
        sums_of(i)
        ex_start(i)

    def pass_on():
        for i in range(last):
            row_start(i, ex_sum(i, part_buf[i, group]))

    when_inside(1, pass_on)
    total_buf[...] = ex_sum(last, part_buf[last, group])
    for i in reversed(range(last)):
        row_copy(i, i).wait_recv()
        total_buf[...] = total_buf[...] + row_in[i].astype(jnp.float32)

        def add_cross(i=i):
            for n in range(groups - 1):
                cross_copy(i, n, i).wait_recv()
                total_buf[...] = total_buf[...] + cross_in[i, n].astype(jnp.float32)

        if four and i == 0:
            add_cross()
        elif four and i == 2:
            when_inside(1, add_cross)
    low = (total_buf[...] * norm_scale).astype(jnp.bfloat16)

    def mate_copy(n):
        return pltpu.make_async_remote_copy(
            src_ref=keep_buf.at[n, 1 - core],
            dst_ref=mate_buf.at[n],
            send_sem=mate_send.at[n],
            recv_sem=mate_recv.at[n],
            device_id={"ex": mate},
            device_id_type=mesh_id,
        )

    def score_copy(n, slot):
        return pltpu.make_async_remote_copy(
            src_ref=score_out.at[n],
            dst_ref=score_in.at[slot],
            send_sem=score_send.at[n],
            recv_sem=score_recv.at[slot],
            device_id={"rows": score_row(n)},
            device_id_type=mesh_id,
        )

    tile = min(own, 512)
    owned = examples // ex_count

    def score_block(n):
        inv_copy(n).wait()
        for j in range(own // tile):
            at = slice(j * tile, (j + 1) * tile)
            got = jnp.dot(low, inv_buf[n, :, at], preferred_element_type=jnp.float32)
            keep_buf[n, :, :, at] = got.reshape(2, owned, tile)
        mate_copy(n).start()

    def score_sum(n):
        mate_copy(n).wait_recv()
        return keep_buf[n, core] + mate_buf[n]

    for n in range(row_count):
        score_block(n)
        if n >= 1:
            score_out[n - 1] = score_sum(n - 1).astype(score_out.dtype)
            score_copy(n - 1, row - 1 + jnp.minimum(jnp.maximum(score_row(n - 1) - row, 0), 1)).start()
    total = score_sum(last)
    for n in range(last):
        score_copy(n, n).wait_recv()
        total = total + score_in[n].astype(jnp.float32)
    out_ref[...] = total.astype(out_ref.dtype)

    cot_copy().wait_send()
    for n in range(row_count):
        relay_copy(n).wait_send()
        mate_copy(n).wait_send()
        for m in range(groups - 1):
            if n == last:
                ex_copy(n, m).wait_send()
            else:
                when_inside(1, ex_copy(n, m).wait_send)
                when_inside(0, cross_copy(n, m, n).wait_send)
    for n in range(last):
        hid_copy(n, n).wait_send()
        row_copy(n, n).wait_send()
        score_copy(n, n).wait_send()


def pair_call(row_count, ex_count, norm_scale, operands):
    hidden_acts, cotangent, lengths, frow = operands[0], operands[1], operands[2], operands[5]
    tok_dev, width = hidden_acts.shape
    cot_width = cotangent.shape[1]
    examples = lengths.shape[1]
    features = frow.shape[1]
    own = features // row_count
    half = own // 2
    groups = ex_count // 2
    owned = examples // ex_count
    last, others = row_count - 1, max(groups - 1, 1)
    dma = pltpu.SemaphoreType.DMA
    low, wide, whole = jnp.bfloat16, jnp.float32, jnp.int32
    vmem = pltpu.VMEM
    return pl.pallas_call(
        functools.partial(pair_kernel, row_count, ex_count, norm_scale),
        out_shape=jax.ShapeDtypeStruct((owned, own), low),
        in_specs=[pl.BlockSpec(memory_space=pltpu.HBM)] * 8,
        out_specs=pl.BlockSpec(memory_space=pltpu.VMEM),
        scratch_shapes=[
            vmem((tok_dev, width), low),
            vmem((tok_dev, cot_width), low),
            vmem((1, examples), whole),
            vmem((1, width), whole),
            vmem((1, cot_width), whole),
            vmem((1, features), whole),
            vmem((1, features), whole),
            vmem((2, row_count, tok_dev, width), low),
            vmem((2, tok_dev, cot_width), low),
            vmem((row_count * width, row_count * half), low),
            vmem((2, tok_dev, row_count * half), wide),
            vmem((2 * tok_dev, row_count * half), low),
            vmem((2 * tok_dev, row_count * half), low),
            vmem((row_count, groups, examples // groups, half), wide),
            vmem((row_count, others, examples // groups, half), low),
            vmem((row_count, others, examples // groups, half), low),
            vmem((last, others, examples // groups, half), low),
            vmem((examples // groups, half), wide),
            vmem((last, examples // groups, half), low),
            vmem((last, examples // groups, half), low),
            vmem((row_count, 2, owned, own), wide),
            vmem((row_count, owned, own), wide),
            vmem((last, owned, own), low),
            vmem((last, owned, own), low),
            vmem((row_count, half, own), low),
            dma((7,)),
            dma((row_count,)),
            dma((last,)),
            dma((last,)),
            dma((row_count,)),
            dma((row_count,)),
            dma,
            dma,
            dma((row_count, others)),
            dma((row_count, others)),
            dma((last, others)),
            dma((last, others)),
            dma((last,)),
            dma((last,)),
            dma((row_count,)),
            dma((row_count,)),
            dma((last,)),
            dma((last,)),
        ],
        compiler_params=pltpu.CompilerParams(
            collective_id=0, has_side_effects=True, vmem_limit_bytes=48 * 1024 * 1024
        ),
        name="features_and_scores",
    )(*[pltpu.with_memory_space_constraint(operand, pltpu.HBM) for operand in operands])


def local(hidden_acts, cotangent, lengths, row_signs, col_signs, feat_row, feat_col, inverse_rows):
    row_count = lax.axis_size("rows")
    ex_count = lax.axis_size("ex")
    tok_dev, width = hidden_acts.shape
    cot_width = cotangent.shape[1]
    features = feat_row.shape[0]
    examples = lengths.shape[0]
    own = features // row_count
    owned = examples // ex_count
    norm_scale = 1.0 / math.sqrt(width * row_count * col_signs.shape[0])
    operands = (
        hidden_acts,
        cotangent,
        lengths.reshape(1, -1),
        row_signs.reshape(1, -1),
        col_signs.reshape(1, -1),
        feat_row.reshape(1, -1),
        feat_col.reshape(1, -1),
        inverse_rows,
    )
    if (
        ex_count % 2 == 0
        and row_count in (2, 4, 8)
        and own % 256 == 0
        and cot_width % 128 == 0
        and width % 128 == 0
        and tok_dev % 16 == 0
        and owned % 8 == 0
        and features * (width * row_count + cot_width + own) <= 32 * 1024 * 1024
    ):
        return pair_call(row_count, ex_count, norm_scale, operands)
    if cot_width % 128 != 0:
        col_signs = lax.dynamic_slice(col_signs, (lax.axis_index("rows") * cot_width,), (cot_width,))
    vmem = pl.BlockSpec(memory_space=pltpu.VMEM)
    others = max(row_count - 1, 1)
    dma = pltpu.SemaphoreType.DMA
    return pl.pallas_call(
        functools.partial(kernel, row_count, ex_count, norm_scale),
        out_shape=jax.ShapeDtypeStruct((owned, own), jnp.bfloat16),
        in_specs=[vmem] * 7 + [pl.BlockSpec(memory_space=pl.ANY)],
        out_specs=vmem,
        scratch_shapes=[
            pltpu.VMEM((row_count, tok_dev, width), jnp.bfloat16),
            pltpu.VMEM((tok_dev, cot_width), jnp.bfloat16),
            pltpu.VMEM((row_count, tok_dev, own), jnp.float32),
            pltpu.VMEM((row_count, ex_count, owned, own), jnp.float32),
            pltpu.VMEM((row_count, max(ex_count - 1, 1), owned, own), jnp.float32),
            pltpu.VMEM((others, owned, own), jnp.bfloat16),
            pltpu.VMEM((others, owned, own), jnp.bfloat16),
            pltpu.VMEM((others, owned, own), jnp.bfloat16),
            pltpu.VMEM((others, owned, own), jnp.bfloat16),
            pltpu.VMEM((row_count, own, own), jnp.bfloat16),
            pltpu.VMEM((owned, own), jnp.float32),
            dma((row_count,)),
            dma((others,)),
            dma((others,)),
            dma((row_count, max(ex_count - 1, 1))),
            dma((row_count, max(ex_count - 1, 1))),
            dma((others,)),
            dma((others,)),
            dma((others,)),
            dma((others,)),
        ],
        compiler_params=pltpu.CompilerParams(
            collective_id=0, has_side_effects=True, vmem_limit_bytes=60 * 1024 * 1024
        ),
        name="features_and_scores",
    )(
        hidden_acts,
        cotangent,
        lengths.reshape(1, -1),
        row_signs.reshape(1, -1),
        col_signs.reshape(1, -1),
        feat_row.reshape(1, -1),
        feat_col.reshape(1, -1),
        inverse_rows,
    )


def solution(mesh):
    placed = (
        P(("parts", "ex"), "rows"),
        P(("parts", "ex"), "rows"),
        P("parts"),
        P("rows"),
        P(),
        P(),
        P(),
        P("rows", None),
    )
    return jax.shard_map(
        local, mesh=mesh, in_specs=placed, out_specs=P(("parts", "ex"), "rows"), check_vma=False
    )
```

```python
import functools
import math

import jax
import jax.numpy as jnp
from jax import lax
from jax.experimental import pallas as pl
from jax.experimental.pallas import tpu as pltpu
from jax.sharding import PartitionSpec as P


def signs(first_bits, second_bits):
    odd = lax.population_count(first_bits & second_bits) & 1
    return (1 - 2 * odd).astype(jnp.float32).astype(jnp.bfloat16)


def sign_rows(first, count, step, picks):
    inner = lax.broadcasted_iota(jnp.int32, (step, picks.shape[1]), 0)
    table = signs(inner, picks)
    parts = [table * signs(jnp.zeros_like(picks) + (first + n * step), picks) for n in range(count)]
    return parts[0] if count == 1 else jnp.concatenate(parts, axis=0)


def loop(count, body):
    if count <= 4:
        for n in range(count):
            body(n)
    else:
        lax.fori_loop(0, count, lambda n, c: (body(n), c)[1], 0)


def when(cond, body):
    if isinstance(cond, bool):
        if cond:
            body()
    else:
        pl.when(cond)(body)


def kernel(
    row_count,
    ex_count,
    norm_scale,
    hid_ref,
    cot_ref,
    len_ref,
    rsign_ref,
    csign_ref,
    frow_ref,
    fcol_ref,
    inv_ref,
    out_ref,
    hid_all,
    cot_signed,
    right_buf,
    part_buf,
    ex_in,
    row_out,
    row_in,
    score_out,
    score_in,
    inv_buf,
    total_buf,
    inv_sem,
    hid_send,
    hid_recv,
    ex_send,
    ex_recv,
    row_send,
    row_recv,
    score_send,
    score_recv,
):
    row = lax.axis_index("rows")
    ex = lax.axis_index("ex")
    tok_dev, width = hid_ref.shape
    cot_width = cot_ref.shape[1]
    features = frow_ref.shape[1]
    own = features // row_count
    examples = len_ref.shape[1]
    chunk = min(own, 512)
    ex_steps = ex_count.bit_length() - 1

    def block_of(i):
        return lax.rem(row + 1 + i, row_count)

    def inv_copy(n):
        cols = pl.ds(pl.multiple_of(block_of(n) * own, 128), own)
        return pltpu.make_async_copy(inv_ref.at[:, cols], inv_buf.at[n], inv_sem.at[n])

    barrier = pltpu.get_barrier_semaphore()

    def greet(n):
        pl.semaphore_signal(
            barrier,
            inc=1,
            device_id={"rows": lax.rem(row + n + 1, row_count)},
            device_id_type=pl.DeviceIdType.MESH,
        )

    loop(row_count - 1, greet)

    def bit_of(step):
        return lax.rem(ex // (1 << step), 2)

    def partner_of(step):
        return ex + (1 - 2 * bit_of(step)) * (1 << step)

    for step in range(ex_steps):
        pl.semaphore_signal(
            barrier,
            inc=1,
            device_id={"ex": partner_of(step)},
            device_id_type=pl.DeviceIdType.MESH,
        )
    loop(row_count, lambda n: inv_copy(n).start())
    hid_all[row] = hid_ref[...] * rsign_ref[...].astype(jnp.float32).astype(jnp.bfloat16)
    if csign_ref.shape[1] == cot_width:
        col_sign = csign_ref[...]
    else:
        col_sign = csign_ref[:, pl.ds(pl.multiple_of(row * cot_width, 128), cot_width)]
    cot_signed[...] = cot_ref[...] * col_sign.astype(jnp.float32).astype(jnp.bfloat16)
    lens = jnp.broadcast_to(len_ref[...].astype(jnp.float32), (examples, examples))
    e_row = lax.broadcasted_iota(jnp.int32, (examples, examples), 0)
    e_col = lax.broadcasted_iota(jnp.int32, (examples, examples), 1)
    ends = jnp.sum(jnp.where(e_col <= e_row, lens, 0.0), axis=1, keepdims=True)
    starts = jnp.sum(jnp.where(e_col < e_row, lens, 0.0), axis=1, keepdims=True)
    spots = ex * tok_dev + lax.broadcasted_iota(jnp.int32, (examples, tok_dev), 1)
    spots = spots.astype(jnp.float32)
    member = jnp.where((spots >= starts) & (spots < ends), 1.0, 0.0).astype(jnp.bfloat16)
    pl.semaphore_wait(barrier, row_count - 1 + ex_steps)

    def hid_copy(n, incoming=False):
        to = lax.rem(row + n + 1, row_count)
        block = lax.rem(row - n - 1 + row_count, row_count) if incoming else row
        return pltpu.make_async_remote_copy(
            src_ref=hid_all.at[block],
            dst_ref=hid_all.at[block],
            send_sem=hid_send.at[n],
            recv_sem=hid_recv.at[n],
            device_id={"rows": to},
            device_id_type=pl.DeviceIdType.MESH,
        )

    loop(row_count - 1, lambda n: hid_copy(n).start())

    def picks_of(ref, i, c):
        at = pl.multiple_of(block_of(i) * own + c * chunk, 128)
        return ref[:, pl.ds(at, chunk)]

    inner = min(cot_width, 128)

    def right_side(i):
        def one(c):
            table = sign_rows(row * cot_width, cot_width // inner, inner, picks_of(fcol_ref, i, c))
            at = c * chunk if isinstance(c, int) else pl.multiple_of(c * chunk, 128)
            right_buf[i, :, pl.ds(at, chunk)] = jnp.dot(
                cot_signed[...], table, preferred_element_type=jnp.float32
            )

        loop(own // chunk, one)

    group = min(row_count, 4)

    def features_of(i):
        def one(c):
            picks = picks_of(frow_ref, i, c)

            def some(g, left):
                acts = jnp.concatenate([hid_all[g * group + n] for n in range(group)], axis=1)
                table = sign_rows(g * group * width, group, width, picks)
                return left + jnp.dot(acts, table, preferred_element_type=jnp.float32)

            left = jnp.zeros((tok_dev, chunk), jnp.float32)
            if row_count == group:
                left = some(0, left)
            else:
                left = lax.fori_loop(0, row_count // group, some, left)
            at = c * chunk if isinstance(c, int) else pl.multiple_of(c * chunk, 128)
            products = left * right_buf[i, :, pl.ds(at, chunk)]
            high = products.astype(jnp.bfloat16)
            rest = (products - high.astype(jnp.float32)).astype(jnp.bfloat16)
            sums = jnp.dot(member, high, preferred_element_type=jnp.float32)
            sums = sums + jnp.dot(member, rest, preferred_element_type=jnp.float32)
            part_buf[i, :, :, pl.ds(at, chunk)] = sums.reshape(ex_count, examples // ex_count, chunk)

        loop(own // chunk, one)

    def ex_copies(i, step):
        size = 1 << step
        first = ex_count - (ex_count >> step)
        copies = []
        for m in range(ex_count >> (step + 1)):
            away = lax.rem(ex, size) + (1 - bit_of(step)) * size + m * 2 * size
            slot = first + m
            copies.append(
                pltpu.make_async_remote_copy(
                    src_ref=part_buf.at[i, away],
                    dst_ref=ex_in.at[i, slot],
                    send_sem=ex_send.at[i, slot],
                    recv_sem=ex_recv.at[i, slot],
                    device_id={"ex": partner_of(step)},
                    device_id_type=pl.DeviceIdType.MESH,
                )
            )
        return copies

    def ex_start(i, step):
        for copy in ex_copies(i, step):
            copy.start()

    def ex_finish(i, step):
        size = 1 << step
        first = ex_count - (ex_count >> step)
        for m, copy in enumerate(ex_copies(i, step)):
            copy.wait_recv()
            mine = lax.rem(ex, 2 * size) + m * 2 * size
            part_buf[i, mine] = part_buf[i, mine] + ex_in[i, first + m]

    def row_copy(i):
        return pltpu.make_async_remote_copy(
            src_ref=row_out.at[i],
            dst_ref=row_in.at[i],
            send_sem=row_send.at[i],
            recv_sem=row_recv.at[i],
            device_id={"rows": block_of(i)},
            device_id_type=pl.DeviceIdType.MESH,
        )

    def stage(i, step):
        def work():
            if step > 0:
                ex_finish(i, step - 1)
            if step < ex_steps:
                ex_start(i, step)
            else:


                def send():
                    row_out[i] = part_buf[i, ex].astype(row_out.dtype)
                    row_copy(i).start()

                when(i < row_count - 1, send)

        return work

    loop(row_count, right_side)
    loop(row_count - 1, lambda n: hid_copy(n, True).wait_recv())

    def block_step(i):
        features_of(i)
        stage(i, 0)()
        for step in range(1, ex_steps + 1):
            when(i >= step, stage(i - step, step))

    loop(row_count, block_step)
    for late in range(1, ex_steps + 1):
        for step in range(late, ex_steps + 1):
            if row_count - 1 + late - step >= 0:
                stage(row_count - 1 + late - step, step)()

    total_buf[...] = part_buf[row_count - 1, ex]

    def add_row(n):
        row_copy(n).wait_recv()
        total_buf[...] = total_buf[...] + row_in[n].astype(jnp.float32)

    loop(row_count - 1, add_row)
    low = (total_buf[...] * norm_scale).astype(jnp.bfloat16)

    def score_copy(n):
        return pltpu.make_async_remote_copy(
            src_ref=score_out.at[n],
            dst_ref=score_in.at[n],
            send_sem=score_send.at[n],
            recv_sem=score_recv.at[n],
            device_id={"rows": block_of(n)},
            device_id_type=pl.DeviceIdType.MESH,
        )

    tile = min(own, 512)

    def score_block(n):
        inv_copy(n).wait()

        def one(j):
            at = j * tile if isinstance(j, int) else pl.multiple_of(j * tile, 128)
            got = jnp.dot(low, inv_buf[n, :, pl.ds(at, tile)], preferred_element_type=jnp.float32)

            def keep():
                total_buf[:, pl.ds(at, tile)] = got

            def give():
                score_out[n, :, pl.ds(at, tile)] = got.astype(score_out.dtype)

            when(n == row_count - 1, keep)
            when(n < row_count - 1, give)

        loop(own // tile, one)
        when(n < row_count - 1, lambda: score_copy(n).start())

    loop(row_count, score_block)
    def add_score(n):
        score_copy(n).wait_recv()
        total_buf[...] = total_buf[...] + score_in[n].astype(jnp.float32)

    loop(row_count - 1, add_score)
    out_ref[...] = total_buf[...].astype(out_ref.dtype)
    loop(row_count - 1, lambda n: hid_copy(n).wait_send())
    loop(row_count - 1, lambda n: score_copy(n).wait_send())
    loop(row_count - 1, lambda n: row_copy(n).wait_send())

    def ex_sent(i):
        for step in range(ex_steps):
            for copy in ex_copies(i, step):
                copy.wait_send()

    loop(row_count, ex_sent)


def pair_kernel(
    row_count,
    ex_count,
    norm_scale,
    hid_hbm,
    cot_hbm,
    len_hbm,
    rsign_hbm,
    csign_hbm,
    frow_hbm,
    fcol_hbm,
    inv_ref,
    out_ref,
    hid_buf,
    cot_buf,
    len_buf,
    rsign_buf,
    csign_buf,
    frow_buf,
    fcol_buf,
    hid_all,
    cot_all,
    left_table,
    right_buf,
    high_buf,
    rest_buf,
    part_buf,
    ex_out,
    ex_in,
    cross_in,
    total_buf,
    row_out,
    row_in,
    keep_buf,
    mate_buf,
    score_out,
    score_in,
    inv_buf,
    load_sem,
    inv_sem,
    hid_send,
    hid_recv,
    relay_send,
    relay_recv,
    cot_send,
    cot_recv,
    ex_send,
    ex_recv,
    cross_send,
    cross_recv,
    row_send,
    row_recv,
    mate_send,
    mate_recv,
    score_send,
    score_recv,
):
    row = lax.axis_index("rows")
    ex = lax.axis_index("ex")
    core = lax.rem(ex, 2)
    mate = ex + 1 - 2 * core
    group = ex // 2
    groups = ex_count // 2
    tok_dev, width = hid_hbm.shape
    cot_width = cot_hbm.shape[1]
    features = frow_hbm.shape[1]
    own = features // row_count
    half = own // 2
    examples = len_hbm.shape[1]
    chunk = min(half, 512)
    mesh_id = pl.DeviceIdType.MESH
    last = row_count - 1
    four = row_count == 4
    inside = lax.rem(row + 1, 4) // 2 if four else 1
    orders = ((3, 2, 1, 0), (2, 3, 1, 0)) if four else (tuple(range(last, -1, -1)),) * 2

    def pick(outer, inner):
        return outer + inside * (inner - outer)

    def flip(mask):
        at = row
        for bit in range(row_count.bit_length() - 1):
            if mask >> bit & 1:
                at = at + (1 - 2 * lax.rem(row // (1 << bit), 2)) * (1 << bit)
        return at

    def other_row(n):
        outer, inner = orders[0][n], orders[1][n]
        return flip(outer) if outer == inner else pick(flip(outer), flip(inner))

    def slot_there(n):
        if not four:
            return n
        return pick(orders[1 if orders[0][n] < last else 0].index(orders[0][n]), orders[0 if orders[1][n] < last else 1].index(orders[1][n]))

    def other_group(n):
        return lax.rem(group + 1 + n, groups)

    barrier = pltpu.get_barrier_semaphore()
    for n in range(last):
        pl.semaphore_signal(barrier, inc=1, device_id={"rows": other_row(n)}, device_id_type=mesh_id)
    for n in range(groups - 1):
        pl.semaphore_signal(
            barrier, inc=1, device_id={"ex": 2 * other_group(n) + core}, device_id_type=mesh_id
        )
    pl.semaphore_signal(barrier, inc=1, device_id={"ex": mate}, device_id_type=mesh_id)

    cols = pl.ds(pl.multiple_of(row * cot_width, 128), cot_width)
    loads = {
        name: pltpu.make_async_copy(source, target, load_sem.at[n])
        for n, (name, source, target) in enumerate(
            (
                ("hid", hid_hbm, hid_buf),
                ("rsign", rsign_hbm, rsign_buf),
                ("cot", cot_hbm, cot_buf),
                ("csign", csign_hbm.at[:, cols], csign_buf),
                ("fcol", fcol_hbm, fcol_buf),
                ("frow", frow_hbm, frow_buf),
                ("len", len_hbm, len_buf),
            )
        )
    }
    for load in loads.values():
        load.start()

    def score_row(n):
        return row if n == last else n + 1 - jnp.minimum(jnp.maximum(row - n, 0), 1)

    def inv_copy(n):
        target = pl.ds(pl.multiple_of(score_row(n) * own, 128), own)
        source = pl.ds(pl.multiple_of(core * half, 16), half)
        return pltpu.make_async_copy(inv_ref.at[source, target], inv_buf.at[n], inv_sem.at[n])

    def picks_of(ref, i, c):
        at = pl.multiple_of(other_row(i) * own + core * half + c * chunk, 128)
        return ref[:, pl.ds(at, chunk)]

    def spot(i, c):
        return slice(i * half + c * chunk, i * half + (c + 1) * chunk)

    loads["hid"].wait()
    loads["rsign"].wait()
    hid_all[0, last] = hid_buf[...] * rsign_buf[...].astype(jnp.float32).astype(jnp.bfloat16)
    loads["cot"].wait()
    loads["csign"].wait()
    cot_all[0] = cot_buf[...] * csign_buf[...].astype(jnp.float32).astype(jnp.bfloat16)
    loads["fcol"].wait()

    def short_rows(first, rows, picks):
        step = min(rows, 16)
        table = signs(lax.broadcasted_iota(jnp.int32, (step, chunk), 0), picks)
        table = table * signs(jnp.zeros_like(picks) + first, picks)
        blocks = signs(lax.broadcasted_iota(jnp.int32, (rows // step, chunk), 0) * step, picks)
        return jnp.concatenate([table * blocks[n : n + 1] for n in range(rows // step)], axis=0)

    def table_of(i, c):
        return short_rows(row * cot_width, cot_width, picks_of(fcol_buf, i, c))

    def right_first(i):
        for c in range(half // chunk):
            table = table_of(i, c)
            right_buf[0, :, spot(i, c)] = jnp.dot(
                cot_all[0], table, preferred_element_type=jnp.float32
            )

    def right_mate(i):
        for c in range(half // chunk):
            right_buf[1, :, spot(i, c)] = jnp.dot(
                cot_all[1], table_of(i, c), preferred_element_type=jnp.float32
            )

    def hid_copy(n, slot):
        return pltpu.make_async_remote_copy(
            src_ref=hid_all.at[0, last],
            dst_ref=hid_all.at[0, slot],
            send_sem=hid_send.at[n],
            recv_sem=hid_recv.at[slot],
            device_id={"rows": other_row(n)},
            device_id_type=mesh_id,
        )

    def relay_copy(n):
        return pltpu.make_async_remote_copy(
            src_ref=hid_all.at[0, n],
            dst_ref=hid_all.at[1, n],
            send_sem=relay_send.at[n],
            recv_sem=relay_recv.at[n],
            device_id={"ex": mate},
            device_id_type=mesh_id,
        )

    def cot_copy():
        return pltpu.make_async_remote_copy(
            src_ref=cot_all.at[0],
            dst_ref=cot_all.at[1],
            send_sem=cot_send,
            recv_sem=cot_recv,
            device_id={"ex": mate},
            device_id_type=mesh_id,
        )

    def enter():
        pl.semaphore_wait(barrier, last + groups)
        for n in range(last):
            hid_copy(n, slot_there(n)).start()
        relay_copy(last).start()

    pl.when(row == last)(enter)
    early = row_count // 2
    for i in range(early):
        right_first(i)
    pl.when(row < last)(enter)
    cot_copy().start()

    loads["len"].wait()
    lens = jnp.broadcast_to(len_buf[...].astype(jnp.float32), (examples, examples))
    e_row = lax.broadcasted_iota(jnp.int32, (examples, examples), 0)
    e_col = lax.broadcasted_iota(jnp.int32, (examples, examples), 1)
    ends = jnp.sum(jnp.where(e_col <= e_row, lens, 0.0), axis=1, keepdims=True)
    starts = jnp.sum(jnp.where(e_col < e_row, lens, 0.0), axis=1, keepdims=True)

    spots = lax.broadcasted_iota(jnp.int32, (examples, 2 * tok_dev), 1)
    mates = (1 - 2 * core) * tok_dev
    spots = jnp.where(spots < tok_dev, spots, spots - tok_dev + mates) + ex * tok_dev
    spots = spots.astype(jnp.float32)
    member = jnp.where((spots >= starts) & (spots < ends), 1.0, 0.0).astype(jnp.bfloat16)

    for i in range(early, row_count):
        right_first(i)
    loads["frow"].wait()
    for i in range(row_count):
        for c in range(half // chunk):
            picks = picks_of(frow_buf, i, c)
            for n in range(row_count):
                rows = slice(n * width, (n + 1) * width)
                left_table[rows, spot(i, c)] = short_rows(other_row(n) * width, width, picks)

    cot_copy().wait_recv()
    for i in range(row_count):
        right_mate(i)

    for n in range(last):
        hid_copy(n, n).wait_recv()
        relay_copy(n).start()
    for n in range(row_count):
        inv_copy(n).start()

    def acts_of(side):
        return jnp.concatenate([hid_all[side, n] for n in range(row_count)], axis=1)

    def products_of(side, i, acts):
        tokens = slice(side * tok_dev, (side + 1) * tok_dev)
        for c in range(half // chunk):
            left = jnp.dot(acts, left_table[:, spot(i, c)], preferred_element_type=jnp.float32)
            products = left * right_buf[side, :, spot(i, c)]
            high = products.astype(jnp.bfloat16)
            high_buf[tokens, spot(i, c)] = high
            rest_buf[tokens, spot(i, c)] = (products - high.astype(jnp.float32)).astype(jnp.bfloat16)

    def sums_of(i):
        at = slice(i * half, (i + 1) * half)
        sums = jnp.dot(member, high_buf[:, at], preferred_element_type=jnp.float32)
        sums = sums + jnp.dot(member, rest_buf[:, at], preferred_element_type=jnp.float32)
        part_buf[i] = sums.reshape(groups, examples // groups, half)

    def ex_copy(i, n):
        return pltpu.make_async_remote_copy(
            src_ref=ex_out.at[i, n],
            dst_ref=ex_in.at[i, n],
            send_sem=ex_send.at[i, n],
            recv_sem=ex_recv.at[i, n],
            device_id={"ex": 2 * other_group(n) + core},
            device_id_type=mesh_id,
        )

    def cross_copy(i, n, slot):
        return pltpu.make_async_remote_copy(
            src_ref=ex_out.at[i, n],
            dst_ref=cross_in.at[slot, n],
            send_sem=cross_send.at[i, n],
            recv_sem=cross_recv.at[slot, n],
            device_id={"rows": other_row(i), "ex": 2 * other_group(n) + core},
            device_id_type=mesh_id,
        )

    def when_inside(is_inside, body):
        if four:
            pl.when(inside == is_inside)(body)
        elif is_inside:
            body()

    def row_copy(i, slot):
        return pltpu.make_async_remote_copy(
            src_ref=row_out.at[i],
            dst_ref=row_in.at[slot],
            send_sem=row_send.at[i],
            recv_sem=row_recv.at[slot],
            device_id={"rows": other_row(i)},
            device_id_type=mesh_id,
        )

    def row_start(i, total):
        row_out[i] = total.astype(row_out.dtype)
        row_copy(i, slot_there(i)).start()

    def two_phase(i):
        for n in range(groups - 1):
            ex_copy(i, n).start()

    def one_phase(i):
        for n in range(groups - 1):
            cross_copy(i, n, slot_there(i)).start()
        row_start(i, part_buf[i, group])

    def ex_start(i):
        for n in range(groups - 1):
            ex_out[i, n] = part_buf[i, other_group(n)].astype(ex_out.dtype)
        if i == last:
            two_phase(i)
        else:
            when_inside(1, lambda: two_phase(i))
            when_inside(0, lambda: one_phase(i))

    def ex_sum(i, total):
        for n in range(groups - 1):
            ex_copy(i, n).wait_recv()
            total = total + ex_in[i, n].astype(jnp.float32)
        return total

    acts = acts_of(0)
    for i in range(row_count):
        products_of(0, i, acts)
    for n in range(row_count):
        relay_copy(n).wait_recv()
    acts = acts_of(1)
    for i in range(row_count):
        products_of(1, i, acts)
        sums_of(i)
        ex_start(i)

    def pass_on():
        for i in range(last):
            row_start(i, ex_sum(i, part_buf[i, group]))

    when_inside(1, pass_on)
    total_buf[...] = ex_sum(last, part_buf[last, group])
    for i in reversed(range(last)):
        row_copy(i, i).wait_recv()
        total_buf[...] = total_buf[...] + row_in[i].astype(jnp.float32)

        def add_cross(i=i):
            for n in range(groups - 1):
                cross_copy(i, n, i).wait_recv()
                total_buf[...] = total_buf[...] + cross_in[i, n].astype(jnp.float32)

        if four and i == 0:
            add_cross()
        elif four and i == 2:
            when_inside(1, add_cross)
    low = (total_buf[...] * norm_scale).astype(jnp.bfloat16)

    def mate_copy(n):
        return pltpu.make_async_remote_copy(
            src_ref=keep_buf.at[n, 1 - core],
            dst_ref=mate_buf.at[n],
            send_sem=mate_send.at[n],
            recv_sem=mate_recv.at[n],
            device_id={"ex": mate},
            device_id_type=mesh_id,
        )

    def score_copy(n, slot):
        return pltpu.make_async_remote_copy(
            src_ref=score_out.at[n],
            dst_ref=score_in.at[slot],
            send_sem=score_send.at[n],
            recv_sem=score_recv.at[slot],
            device_id={"rows": score_row(n)},
            device_id_type=mesh_id,
        )

    tile = min(own, 512)
    owned = examples // ex_count

    def score_block(n):
        inv_copy(n).wait()
        for j in range(own // tile):
            at = slice(j * tile, (j + 1) * tile)
            got = jnp.dot(low, inv_buf[n, :, at], preferred_element_type=jnp.float32)
            keep_buf[n, :, :, at] = got.reshape(2, owned, tile)
        mate_copy(n).start()

    def score_sum(n):
        mate_copy(n).wait_recv()
        return keep_buf[n, core] + mate_buf[n]

    for n in range(row_count):
        score_block(n)
        if n >= 1:
            score_out[n - 1] = score_sum(n - 1).astype(score_out.dtype)
            score_copy(n - 1, row - 1 + jnp.minimum(jnp.maximum(score_row(n - 1) - row, 0), 1)).start()
    total = score_sum(last)
    for n in range(last):
        score_copy(n, n).wait_recv()
        total = total + score_in[n].astype(jnp.float32)
    out_ref[...] = total.astype(out_ref.dtype)

    cot_copy().wait_send()
    for n in range(row_count):
        relay_copy(n).wait_send()
        mate_copy(n).wait_send()
        for m in range(groups - 1):
            if n == last:
                ex_copy(n, m).wait_send()
            else:
                when_inside(1, ex_copy(n, m).wait_send)
                when_inside(0, cross_copy(n, m, n).wait_send)
    for n in range(last):
        hid_copy(n, n).wait_send()
        row_copy(n, n).wait_send()
        score_copy(n, n).wait_send()


def pair_call(row_count, ex_count, norm_scale, operands):
    hidden_acts, cotangent, lengths, frow = operands[0], operands[1], operands[2], operands[5]
    tok_dev, width = hidden_acts.shape
    cot_width = cotangent.shape[1]
    examples = lengths.shape[1]
    features = frow.shape[1]
    own = features // row_count
    half = own // 2
    groups = ex_count // 2
    owned = examples // ex_count
    last, others = row_count - 1, max(groups - 1, 1)
    dma = pltpu.SemaphoreType.DMA
    low, wide, whole = jnp.bfloat16, jnp.float32, jnp.int32
    vmem = pltpu.VMEM
    return pl.pallas_call(
        functools.partial(pair_kernel, row_count, ex_count, norm_scale),
        out_shape=jax.ShapeDtypeStruct((owned, own), low),
        in_specs=[pl.BlockSpec(memory_space=pltpu.HBM)] * 8,
        out_specs=pl.BlockSpec(memory_space=pltpu.VMEM),
        scratch_shapes=[
            vmem((tok_dev, width), low),
            vmem((tok_dev, cot_width), low),
            vmem((1, examples), whole),
            vmem((1, width), whole),
            vmem((1, cot_width), whole),
            vmem((1, features), whole),
            vmem((1, features), whole),
            vmem((2, row_count, tok_dev, width), low),
            vmem((2, tok_dev, cot_width), low),
            vmem((row_count * width, row_count * half), low),
            vmem((2, tok_dev, row_count * half), wide),
            vmem((2 * tok_dev, row_count * half), low),
            vmem((2 * tok_dev, row_count * half), low),
            vmem((row_count, groups, examples // groups, half), wide),
            vmem((row_count, others, examples // groups, half), low),
            vmem((row_count, others, examples // groups, half), low),
            vmem((last, others, examples // groups, half), low),
            vmem((examples // groups, half), wide),
            vmem((last, examples // groups, half), low),
            vmem((last, examples // groups, half), low),
            vmem((row_count, 2, owned, own), wide),
            vmem((row_count, owned, own), wide),
            vmem((last, owned, own), low),
            vmem((last, owned, own), low),
            vmem((row_count, half, own), low),
            dma((7,)),
            dma((row_count,)),
            dma((last,)),
            dma((last,)),
            dma((row_count,)),
            dma((row_count,)),
            dma,
            dma,
            dma((row_count, others)),
            dma((row_count, others)),
            dma((last, others)),
            dma((last, others)),
            dma((last,)),
            dma((last,)),
            dma((row_count,)),
            dma((row_count,)),
            dma((last,)),
            dma((last,)),
        ],
        compiler_params=pltpu.CompilerParams(
            collective_id=0, has_side_effects=True, vmem_limit_bytes=48 * 1024 * 1024
        ),
        name="features_and_scores",
    )(*[pltpu.with_memory_space_constraint(operand, pltpu.HBM) for operand in operands])


def local(hidden_acts, cotangent, lengths, row_signs, col_signs, feat_row, feat_col, inverse_rows):
    row_count = lax.axis_size("rows")
    ex_count = lax.axis_size("ex")
    tok_dev, width = hidden_acts.shape
    cot_width = cotangent.shape[1]
    features = feat_row.shape[0]
    examples = lengths.shape[0]
    own = features // row_count
    owned = examples // ex_count
    norm_scale = 1.0 / math.sqrt(width * row_count * col_signs.shape[0])
    operands = (
        hidden_acts,
        cotangent,
        lengths.reshape(1, -1),
        row_signs.reshape(1, -1),
        col_signs.reshape(1, -1),
        feat_row.reshape(1, -1),
        feat_col.reshape(1, -1),
        inverse_rows,
    )
    if (
        ex_count % 2 == 0
        and row_count in (2, 4, 8)
        and own % 256 == 0
        and cot_width % 128 == 0
        and width % 128 == 0
        and tok_dev % 16 == 0
        and owned % 8 == 0
        and features * (width * row_count + cot_width + own) <= 32 * 1024 * 1024
    ):
        return pair_call(row_count, ex_count, norm_scale, operands)
    if cot_width % 128 != 0:
        col_signs = lax.dynamic_slice(col_signs, (lax.axis_index("rows") * cot_width,), (cot_width,))
    vmem = pl.BlockSpec(memory_space=pltpu.VMEM)
    others = max(row_count - 1, 1)
    dma = pltpu.SemaphoreType.DMA
    return pl.pallas_call(
        functools.partial(kernel, row_count, ex_count, norm_scale),
        out_shape=jax.ShapeDtypeStruct((owned, own), jnp.bfloat16),
        in_specs=[vmem] * 7 + [pl.BlockSpec(memory_space=pl.ANY)],
        out_specs=vmem,
        scratch_shapes=[
            pltpu.VMEM((row_count, tok_dev, width), jnp.bfloat16),
            pltpu.VMEM((tok_dev, cot_width), jnp.bfloat16),
            pltpu.VMEM((row_count, tok_dev, own), jnp.float32),
            pltpu.VMEM((row_count, ex_count, owned, own), jnp.float32),
            pltpu.VMEM((row_count, max(ex_count - 1, 1), owned, own), jnp.float32),
            pltpu.VMEM((others, owned, own), jnp.bfloat16),
            pltpu.VMEM((others, owned, own), jnp.bfloat16),
            pltpu.VMEM((others, owned, own), jnp.bfloat16),
            pltpu.VMEM((others, owned, own), jnp.bfloat16),
            pltpu.VMEM((row_count, own, own), jnp.bfloat16),
            pltpu.VMEM((owned, own), jnp.float32),
            dma((row_count,)),
            dma((others,)),
            dma((others,)),
            dma((row_count, max(ex_count - 1, 1))),
            dma((row_count, max(ex_count - 1, 1))),
            dma((others,)),
            dma((others,)),
            dma((others,)),
            dma((others,)),
        ],
        compiler_params=pltpu.CompilerParams(
            collective_id=0, has_side_effects=True, vmem_limit_bytes=60 * 1024 * 1024
        ),
        name="features_and_scores",
    )(
        hidden_acts,
        cotangent,
        lengths.reshape(1, -1),
        row_signs.reshape(1, -1),
        col_signs.reshape(1, -1),
        feat_row.reshape(1, -1),
        feat_col.reshape(1, -1),
        inverse_rows,
    )


def solution(mesh):
    placed = (
        P(("parts", "ex"), "rows"),
        P(("parts", "ex"), "rows"),
        P("parts"),
        P("rows"),
        P(),
        P(),
        P(),
        P("rows", None),
    )
    return jax.shard_map(
        local, mesh=mesh, in_specs=placed, out_specs=P(("parts", "ex"), "rows"), check_vma=False
    )
```

```python
import functools
import math

import jax
import jax.numpy as jnp
from jax import lax
from jax.experimental import pallas as pl
from jax.experimental.pallas import tpu as pltpu
from jax.sharding import PartitionSpec as P


def signs(first_bits, second_bits):
    odd = lax.population_count(first_bits & second_bits) & 1
    return (1 - 2 * odd).astype(jnp.float32).astype(jnp.bfloat16)


def sign_rows(first, count, step, picks):
    inner = lax.broadcasted_iota(jnp.int32, (step, picks.shape[1]), 0)
    table = signs(inner, picks)
    parts = [table * signs(jnp.zeros_like(picks) + (first + n * step), picks) for n in range(count)]
    return parts[0] if count == 1 else jnp.concatenate(parts, axis=0)


def loop(count, body):
    if count <= 4:
        for n in range(count):
            body(n)
    else:
        lax.fori_loop(0, count, lambda n, c: (body(n), c)[1], 0)


def when(cond, body):
    if isinstance(cond, bool):
        if cond:
            body()
    else:
        pl.when(cond)(body)


def kernel(
    row_count,
    ex_count,
    norm_scale,
    hid_ref,
    cot_ref,
    len_ref,
    rsign_ref,
    csign_ref,
    frow_ref,
    fcol_ref,
    inv_ref,
    out_ref,
    hid_all,
    cot_signed,
    right_buf,
    part_buf,
    ex_in,
    row_out,
    row_in,
    score_out,
    score_in,
    inv_buf,
    total_buf,
    inv_sem,
    hid_send,
    hid_recv,
    ex_send,
    ex_recv,
    row_send,
    row_recv,
    score_send,
    score_recv,
):
    row = lax.axis_index("rows")
    ex = lax.axis_index("ex")
    tok_dev, width = hid_ref.shape
    cot_width = cot_ref.shape[1]
    features = frow_ref.shape[1]
    own = features // row_count
    examples = len_ref.shape[1]
    chunk = min(own, 512)
    ex_steps = ex_count.bit_length() - 1

    def block_of(i):
        return lax.rem(row + 1 + i, row_count)

    def inv_copy(n):
        cols = pl.ds(pl.multiple_of(block_of(n) * own, 128), own)
        return pltpu.make_async_copy(inv_ref.at[:, cols], inv_buf.at[n], inv_sem.at[n])

    barrier = pltpu.get_barrier_semaphore()

    def greet(n):
        pl.semaphore_signal(
            barrier,
            inc=1,
            device_id={"rows": lax.rem(row + n + 1, row_count)},
            device_id_type=pl.DeviceIdType.MESH,
        )

    loop(row_count - 1, greet)

    def bit_of(step):
        return lax.rem(ex // (1 << step), 2)

    def partner_of(step):
        return ex + (1 - 2 * bit_of(step)) * (1 << step)

    for step in range(ex_steps):
        pl.semaphore_signal(
            barrier,
            inc=1,
            device_id={"ex": partner_of(step)},
            device_id_type=pl.DeviceIdType.MESH,
        )
    loop(row_count, lambda n: inv_copy(n).start())
    hid_all[row] = hid_ref[...] * rsign_ref[...].astype(jnp.float32).astype(jnp.bfloat16)
    if csign_ref.shape[1] == cot_width:
        col_sign = csign_ref[...]
    else:
        col_sign = csign_ref[:, pl.ds(pl.multiple_of(row * cot_width, 128), cot_width)]
    cot_signed[...] = cot_ref[...] * col_sign.astype(jnp.float32).astype(jnp.bfloat16)
    lens = jnp.broadcast_to(len_ref[...].astype(jnp.float32), (examples, examples))
    e_row = lax.broadcasted_iota(jnp.int32, (examples, examples), 0)
    e_col = lax.broadcasted_iota(jnp.int32, (examples, examples), 1)
    ends = jnp.sum(jnp.where(e_col <= e_row, lens, 0.0), axis=1, keepdims=True)
    starts = jnp.sum(jnp.where(e_col < e_row, lens, 0.0), axis=1, keepdims=True)
    spots = ex * tok_dev + lax.broadcasted_iota(jnp.int32, (examples, tok_dev), 1)
    spots = spots.astype(jnp.float32)
    member = jnp.where((spots >= starts) & (spots < ends), 1.0, 0.0).astype(jnp.bfloat16)
    pl.semaphore_wait(barrier, row_count - 1 + ex_steps)

    def hid_copy(n, incoming=False):
        to = lax.rem(row + n + 1, row_count)
        block = lax.rem(row - n - 1 + row_count, row_count) if incoming else row
        return pltpu.make_async_remote_copy(
            src_ref=hid_all.at[block],
            dst_ref=hid_all.at[block],
            send_sem=hid_send.at[n],
            recv_sem=hid_recv.at[n],
            device_id={"rows": to},
            device_id_type=pl.DeviceIdType.MESH,
        )

    loop(row_count - 1, lambda n: hid_copy(n).start())

    def picks_of(ref, i, c):
        at = pl.multiple_of(block_of(i) * own + c * chunk, 128)
        return ref[:, pl.ds(at, chunk)]

    inner = min(cot_width, 128)

    def right_side(i):
        def one(c):
            table = sign_rows(row * cot_width, cot_width // inner, inner, picks_of(fcol_ref, i, c))
            at = c * chunk if isinstance(c, int) else pl.multiple_of(c * chunk, 128)
            right_buf[i, :, pl.ds(at, chunk)] = jnp.dot(
                cot_signed[...], table, preferred_element_type=jnp.float32
            )

        loop(own // chunk, one)

    group = min(row_count, 4)

    def features_of(i):
        def one(c):
            picks = picks_of(frow_ref, i, c)

            def some(g, left):
                acts = jnp.concatenate([hid_all[g * group + n] for n in range(group)], axis=1)
                table = sign_rows(g * group * width, group, width, picks)
                return left + jnp.dot(acts, table, preferred_element_type=jnp.float32)

            left = jnp.zeros((tok_dev, chunk), jnp.float32)
            if row_count == group:
                left = some(0, left)
            else:
                left = lax.fori_loop(0, row_count // group, some, left)
            at = c * chunk if isinstance(c, int) else pl.multiple_of(c * chunk, 128)
            products = left * right_buf[i, :, pl.ds(at, chunk)]
            high = products.astype(jnp.bfloat16)
            rest = (products - high.astype(jnp.float32)).astype(jnp.bfloat16)
            sums = jnp.dot(member, high, preferred_element_type=jnp.float32)
            sums = sums + jnp.dot(member, rest, preferred_element_type=jnp.float32)
            part_buf[i, :, :, pl.ds(at, chunk)] = sums.reshape(ex_count, examples // ex_count, chunk)

        loop(own // chunk, one)

    def ex_copies(i, step):
        size = 1 << step
        first = ex_count - (ex_count >> step)
        copies = []
        for m in range(ex_count >> (step + 1)):
            away = lax.rem(ex, size) + (1 - bit_of(step)) * size + m * 2 * size
            slot = first + m
            copies.append(
                pltpu.make_async_remote_copy(
                    src_ref=part_buf.at[i, away],
                    dst_ref=ex_in.at[i, slot],
                    send_sem=ex_send.at[i, slot],
                    recv_sem=ex_recv.at[i, slot],
                    device_id={"ex": partner_of(step)},
                    device_id_type=pl.DeviceIdType.MESH,
                )
            )
        return copies

    def ex_start(i, step):
        for copy in ex_copies(i, step):
            copy.start()

    def ex_finish(i, step):
        size = 1 << step
        first = ex_count - (ex_count >> step)
        for m, copy in enumerate(ex_copies(i, step)):
            copy.wait_recv()
            mine = lax.rem(ex, 2 * size) + m * 2 * size
            part_buf[i, mine] = part_buf[i, mine] + ex_in[i, first + m]

    def row_copy(i):
        return pltpu.make_async_remote_copy(
            src_ref=row_out.at[i],
            dst_ref=row_in.at[i],
            send_sem=row_send.at[i],
            recv_sem=row_recv.at[i],
            device_id={"rows": block_of(i)},
            device_id_type=pl.DeviceIdType.MESH,
        )

    def stage(i, step):
        def work():
            if step > 0:
                ex_finish(i, step - 1)
            if step < ex_steps:
                ex_start(i, step)
            else:


                def send():
                    row_out[i] = part_buf[i, ex].astype(row_out.dtype)
                    row_copy(i).start()

                when(i < row_count - 1, send)

        return work

    loop(row_count, right_side)
    loop(row_count - 1, lambda n: hid_copy(n, True).wait_recv())

    def block_step(i):
        features_of(i)
        stage(i, 0)()
        for step in range(1, ex_steps + 1):
            when(i >= step, stage(i - step, step))

    loop(row_count, block_step)
    for late in range(1, ex_steps + 1):
        for step in range(late, ex_steps + 1):
            if row_count - 1 + late - step >= 0:
                stage(row_count - 1 + late - step, step)()

    total_buf[...] = part_buf[row_count - 1, ex]

    def add_row(n):
        row_copy(n).wait_recv()
        total_buf[...] = total_buf[...] + row_in[n].astype(jnp.float32)

    loop(row_count - 1, add_row)
    low = (total_buf[...] * norm_scale).astype(jnp.bfloat16)

    def score_copy(n):
        return pltpu.make_async_remote_copy(
            src_ref=score_out.at[n],
            dst_ref=score_in.at[n],
            send_sem=score_send.at[n],
            recv_sem=score_recv.at[n],
            device_id={"rows": block_of(n)},
            device_id_type=pl.DeviceIdType.MESH,
        )

    tile = min(own, 512)

    def score_block(n):
        inv_copy(n).wait()

        def one(j):
            at = j * tile if isinstance(j, int) else pl.multiple_of(j * tile, 128)
            got = jnp.dot(low, inv_buf[n, :, pl.ds(at, tile)], preferred_element_type=jnp.float32)

            def keep():
                total_buf[:, pl.ds(at, tile)] = got

            def give():
                score_out[n, :, pl.ds(at, tile)] = got.astype(score_out.dtype)

            when(n == row_count - 1, keep)
            when(n < row_count - 1, give)

        loop(own // tile, one)
        when(n < row_count - 1, lambda: score_copy(n).start())

    loop(row_count, score_block)
    def add_score(n):
        score_copy(n).wait_recv()
        total_buf[...] = total_buf[...] + score_in[n].astype(jnp.float32)

    loop(row_count - 1, add_score)
    out_ref[...] = total_buf[...].astype(out_ref.dtype)
    loop(row_count - 1, lambda n: hid_copy(n).wait_send())
    loop(row_count - 1, lambda n: score_copy(n).wait_send())
    loop(row_count - 1, lambda n: row_copy(n).wait_send())

    def ex_sent(i):
        for step in range(ex_steps):
            for copy in ex_copies(i, step):
                copy.wait_send()

    loop(row_count, ex_sent)


def pair_kernel(
    row_count,
    ex_count,
    norm_scale,
    hid_hbm,
    cot_hbm,
    len_hbm,
    rsign_hbm,
    csign_hbm,
    frow_hbm,
    fcol_hbm,
    inv_ref,
    out_ref,
    hid_buf,
    cot_buf,
    len_buf,
    rsign_buf,
    csign_buf,
    frow_buf,
    fcol_buf,
    hid_all,
    cot_all,
    left_table,
    right_buf,
    high_buf,
    rest_buf,
    part_buf,
    ex_out,
    ex_in,
    cross_in,
    total_buf,
    row_out,
    row_in,
    keep_buf,
    mate_buf,
    score_out,
    score_in,
    inv_buf,
    load_sem,
    inv_sem,
    hid_send,
    hid_recv,
    relay_send,
    relay_recv,
    cot_send,
    cot_recv,
    ex_send,
    ex_recv,
    cross_send,
    cross_recv,
    row_send,
    row_recv,
    mate_send,
    mate_recv,
    score_send,
    score_recv,
):
    row = lax.axis_index("rows")
    ex = lax.axis_index("ex")
    core = lax.rem(ex, 2)
    mate = ex + 1 - 2 * core
    group = ex // 2
    groups = ex_count // 2
    tok_dev, width = hid_hbm.shape
    cot_width = cot_hbm.shape[1]
    features = frow_hbm.shape[1]
    own = features // row_count
    half = own // 2
    examples = len_hbm.shape[1]
    chunk = min(half, 1024)
    mesh_id = pl.DeviceIdType.MESH
    last = row_count - 1
    four = row_count == 4
    inside = lax.rem(row + 1, 4) // 2 if four else 1
    orders = ((3, 2, 1, 0), (2, 3, 1, 0)) if four else (tuple(range(last, -1, -1)),) * 2

    def pick(outer, inner):
        return outer + inside * (inner - outer)

    def flip(mask):
        at = row
        for bit in range(row_count.bit_length() - 1):
            if mask >> bit & 1:
                at = at + (1 - 2 * lax.rem(row // (1 << bit), 2)) * (1 << bit)
        return at

    def other_row(n):
        outer, inner = orders[0][n], orders[1][n]
        return flip(outer) if outer == inner else pick(flip(outer), flip(inner))

    def slot_there(n):
        if not four:
            return n
        return pick(orders[1 if orders[0][n] < last else 0].index(orders[0][n]), orders[0 if orders[1][n] < last else 1].index(orders[1][n]))

    def other_group(n):
        return lax.rem(group + 1 + n, groups)

    barrier = pltpu.get_barrier_semaphore()
    for n in range(last):
        pl.semaphore_signal(barrier, inc=1, device_id={"rows": other_row(n)}, device_id_type=mesh_id)
    for n in range(groups - 1):
        pl.semaphore_signal(
            barrier, inc=1, device_id={"ex": 2 * other_group(n) + core}, device_id_type=mesh_id
        )
    pl.semaphore_signal(barrier, inc=1, device_id={"ex": mate}, device_id_type=mesh_id)

    cols = pl.ds(pl.multiple_of(row * cot_width, 128), cot_width)
    loads = {
        name: pltpu.make_async_copy(source, target, load_sem.at[n])
        for n, (name, source, target) in enumerate(
            (
                ("hid", hid_hbm, hid_buf),
                ("rsign", rsign_hbm, rsign_buf),
                ("cot", cot_hbm, cot_buf),
                ("csign", csign_hbm.at[:, cols], csign_buf),
                ("fcol", fcol_hbm, fcol_buf),
                ("frow", frow_hbm, frow_buf),
                ("len", len_hbm, len_buf),
            )
        )
    }
    for load in loads.values():
        load.start()

    def score_row(n):
        return row if n == last else n + 1 - jnp.minimum(jnp.maximum(row - n, 0), 1)

    def inv_copy(n):
        target = pl.ds(pl.multiple_of(score_row(n) * own, 128), own)
        source = pl.ds(pl.multiple_of(core * half, 16), half)
        return pltpu.make_async_copy(inv_ref.at[source, target], inv_buf.at[n], inv_sem.at[n])

    def picks_of(ref, i, c):
        at = pl.multiple_of(other_row(i) * own + core * half + c * chunk, 128)
        return ref[:, pl.ds(at, chunk)]

    def spot(i, c):
        return slice(i * half + c * chunk, i * half + (c + 1) * chunk)

    loads["hid"].wait()
    loads["rsign"].wait()
    hid_all[0, last] = hid_buf[...] * rsign_buf[...].astype(jnp.float32).astype(jnp.bfloat16)
    loads["cot"].wait()
    loads["csign"].wait()
    cot_all[0] = cot_buf[...] * csign_buf[...].astype(jnp.float32).astype(jnp.bfloat16)
    loads["fcol"].wait()

    def short_rows(first, rows, picks):
        step = min(rows, 16)
        table = signs(lax.broadcasted_iota(jnp.int32, (step, chunk), 0), picks)
        table = table * signs(jnp.zeros_like(picks) + first, picks)
        blocks = signs(lax.broadcasted_iota(jnp.int32, (rows // step, chunk), 0) * step, picks)
        return jnp.concatenate([table * blocks[n : n + 1] for n in range(rows // step)], axis=0)

    def table_of(i, c):
        return short_rows(row * cot_width, cot_width, picks_of(fcol_buf, i, c))

    def right_first(i):
        for c in range(half // chunk):
            table = table_of(i, c)
            right_buf[0, :, spot(i, c)] = jnp.dot(
                cot_all[0], table, preferred_element_type=jnp.float32
            )

    def right_mate(i):
        for c in range(half // chunk):
            right_buf[1, :, spot(i, c)] = jnp.dot(
                cot_all[1], table_of(i, c), preferred_element_type=jnp.float32
            )

    def hid_copy(n, slot):
        return pltpu.make_async_remote_copy(
            src_ref=hid_all.at[0, last],
            dst_ref=hid_all.at[0, slot],
            send_sem=hid_send.at[n],
            recv_sem=hid_recv.at[slot],
            device_id={"rows": other_row(n)},
            device_id_type=mesh_id,
        )

    def relay_copy(n):
        return pltpu.make_async_remote_copy(
            src_ref=hid_all.at[0, n],
            dst_ref=hid_all.at[1, n],
            send_sem=relay_send.at[n],
            recv_sem=relay_recv.at[n],
            device_id={"ex": mate},
            device_id_type=mesh_id,
        )

    def cot_copy():
        return pltpu.make_async_remote_copy(
            src_ref=cot_all.at[0],
            dst_ref=cot_all.at[1],
            send_sem=cot_send,
            recv_sem=cot_recv,
            device_id={"ex": mate},
            device_id_type=mesh_id,
        )

    early = row_count // 2
    for i in range(early):
        right_first(i)
    pl.semaphore_wait(barrier, last + groups)
    for n in range(last):
        hid_copy(n, slot_there(n)).start()
    relay_copy(last).start()
    cot_copy().start()

    loads["len"].wait()
    lens = jnp.broadcast_to(len_buf[...].astype(jnp.float32), (examples, examples))
    e_row = lax.broadcasted_iota(jnp.int32, (examples, examples), 0)
    e_col = lax.broadcasted_iota(jnp.int32, (examples, examples), 1)
    ends = jnp.sum(jnp.where(e_col <= e_row, lens, 0.0), axis=1, keepdims=True)
    starts = jnp.sum(jnp.where(e_col < e_row, lens, 0.0), axis=1, keepdims=True)

    spots = lax.broadcasted_iota(jnp.int32, (examples, 2 * tok_dev), 1)
    mates = (1 - 2 * core) * tok_dev
    spots = jnp.where(spots < tok_dev, spots, spots - tok_dev + mates) + ex * tok_dev
    spots = spots.astype(jnp.float32)
    member = jnp.where((spots >= starts) & (spots < ends), 1.0, 0.0).astype(jnp.bfloat16)

    for i in range(early, row_count):
        right_first(i)
    loads["frow"].wait()
    for i in range(row_count):
        for c in range(half // chunk):
            picks = picks_of(frow_buf, i, c)
            for n in range(row_count):
                rows = slice(n * width, (n + 1) * width)
                left_table[rows, spot(i, c)] = short_rows(other_row(n) * width, width, picks)

    cot_copy().wait_recv()
    for i in range(row_count):
        right_mate(i)

    for n in range(last):
        hid_copy(n, n).wait_recv()
        relay_copy(n).start()
    for n in range(row_count):
        inv_copy(n).start()

    def acts_of(side):
        return jnp.concatenate([hid_all[side, n] for n in range(row_count)], axis=1)

    def products_of(side, i, acts):
        tokens = slice(side * tok_dev, (side + 1) * tok_dev)
        for c in range(half // chunk):
            left = jnp.dot(acts, left_table[:, spot(i, c)], preferred_element_type=jnp.float32)
            products = left * right_buf[side, :, spot(i, c)]
            high = products.astype(jnp.bfloat16)
            high_buf[tokens, spot(i, c)] = high
            rest_buf[tokens, spot(i, c)] = (products - high.astype(jnp.float32)).astype(jnp.bfloat16)

    def sums_of(i):
        at = slice(i * half, (i + 1) * half)
        sums = jnp.dot(member, high_buf[:, at], preferred_element_type=jnp.float32)
        sums = sums + jnp.dot(member, rest_buf[:, at], preferred_element_type=jnp.float32)
        part_buf[i] = sums.reshape(groups, examples // groups, half)

    def ex_copy(i, n):
        return pltpu.make_async_remote_copy(
            src_ref=ex_out.at[i, n],
            dst_ref=ex_in.at[i, n],
            send_sem=ex_send.at[i, n],
            recv_sem=ex_recv.at[i, n],
            device_id={"ex": 2 * other_group(n) + core},
            device_id_type=mesh_id,
        )

    def cross_copy(i, n, slot):
        return pltpu.make_async_remote_copy(
            src_ref=ex_out.at[i, n],
            dst_ref=cross_in.at[slot, n],
            send_sem=cross_send.at[i, n],
            recv_sem=cross_recv.at[slot, n],
            device_id={"rows": other_row(i), "ex": 2 * other_group(n) + core},
            device_id_type=mesh_id,
        )

    def when_inside(is_inside, body):
        if four:
            pl.when(inside == is_inside)(body)
        elif is_inside:
            body()

    def row_copy(i, slot):
        return pltpu.make_async_remote_copy(
            src_ref=row_out.at[i],
            dst_ref=row_in.at[slot],
            send_sem=row_send.at[i],
            recv_sem=row_recv.at[slot],
            device_id={"rows": other_row(i)},
            device_id_type=mesh_id,
        )

    def row_start(i, total):
        row_out[i] = total.astype(row_out.dtype)
        row_copy(i, slot_there(i)).start()

    def two_phase(i):
        for n in range(groups - 1):
            ex_copy(i, n).start()

    def one_phase(i):
        for n in range(groups - 1):
            cross_copy(i, n, slot_there(i)).start()
        row_start(i, part_buf[i, group])

    def ex_start(i):
        for n in range(groups - 1):
            ex_out[i, n] = part_buf[i, other_group(n)].astype(ex_out.dtype)
        if i == last:
            two_phase(i)
        else:
            when_inside(1, lambda: two_phase(i))
            when_inside(0, lambda: one_phase(i))

    def ex_sum(i, total):
        for n in range(groups - 1):
            ex_copy(i, n).wait_recv()
            total = total + ex_in[i, n].astype(jnp.float32)
        return total

    acts = acts_of(0)
    for i in range(row_count):
        products_of(0, i, acts)
    for n in range(row_count):
        relay_copy(n).wait_recv()
    acts = acts_of(1)
    for i in range(row_count):
        products_of(1, i, acts)
        sums_of(i)
        ex_start(i)

    def pass_on():
        for i in range(last):
            row_start(i, ex_sum(i, part_buf[i, group]))

    when_inside(1, pass_on)
    total_buf[...] = ex_sum(last, part_buf[last, group])
    for i in reversed(range(last)):
        row_copy(i, i).wait_recv()
        total_buf[...] = total_buf[...] + row_in[i].astype(jnp.float32)

        def add_cross(i=i):
            for n in range(groups - 1):
                cross_copy(i, n, i).wait_recv()
                total_buf[...] = total_buf[...] + cross_in[i, n].astype(jnp.float32)

        if four and i == 0:
            add_cross()
        elif four and i == 2:
            when_inside(1, add_cross)
    low = (total_buf[...] * norm_scale).astype(jnp.bfloat16)

    def mate_copy(n):
        return pltpu.make_async_remote_copy(
            src_ref=keep_buf.at[n, 1 - core],
            dst_ref=mate_buf.at[n],
            send_sem=mate_send.at[n],
            recv_sem=mate_recv.at[n],
            device_id={"ex": mate},
            device_id_type=mesh_id,
        )

    def score_copy(n, slot):
        return pltpu.make_async_remote_copy(
            src_ref=score_out.at[n],
            dst_ref=score_in.at[slot],
            send_sem=score_send.at[n],
            recv_sem=score_recv.at[slot],
            device_id={"rows": score_row(n)},
            device_id_type=mesh_id,
        )

    tile = min(own, 512)
    owned = examples // ex_count

    def score_block(n):
        inv_copy(n).wait()
        for j in range(own // tile):
            at = slice(j * tile, (j + 1) * tile)
            got = jnp.dot(low, inv_buf[n, :, at], preferred_element_type=jnp.float32)
            keep_buf[n, :, :, at] = got.reshape(2, owned, tile)
        mate_copy(n).start()

    def score_sum(n):
        mate_copy(n).wait_recv()
        return keep_buf[n, core] + mate_buf[n]

    for n in range(row_count):
        score_block(n)
        if n >= 1:
            score_out[n - 1] = score_sum(n - 1).astype(score_out.dtype)
            score_copy(n - 1, row - 1 + jnp.minimum(jnp.maximum(score_row(n - 1) - row, 0), 1)).start()
    total = score_sum(last)
    for n in range(last):
        score_copy(n, n).wait_recv()
        total = total + score_in[n].astype(jnp.float32)
    out_ref[...] = total.astype(out_ref.dtype)

    cot_copy().wait_send()
    for n in range(row_count):
        relay_copy(n).wait_send()
        mate_copy(n).wait_send()
        for m in range(groups - 1):
            if n == last:
                ex_copy(n, m).wait_send()
            else:
                when_inside(1, ex_copy(n, m).wait_send)
                when_inside(0, cross_copy(n, m, n).wait_send)
    for n in range(last):
        hid_copy(n, n).wait_send()
        row_copy(n, n).wait_send()
        score_copy(n, n).wait_send()


def pair_call(row_count, ex_count, norm_scale, operands):
    hidden_acts, cotangent, lengths, frow = operands[0], operands[1], operands[2], operands[5]
    tok_dev, width = hidden_acts.shape
    cot_width = cotangent.shape[1]
    examples = lengths.shape[1]
    features = frow.shape[1]
    own = features // row_count
    half = own // 2
    groups = ex_count // 2
    owned = examples // ex_count
    last, others = row_count - 1, max(groups - 1, 1)
    dma = pltpu.SemaphoreType.DMA
    low, wide, whole = jnp.bfloat16, jnp.float32, jnp.int32
    vmem = pltpu.VMEM
    return pl.pallas_call(
        functools.partial(pair_kernel, row_count, ex_count, norm_scale),
        out_shape=jax.ShapeDtypeStruct((owned, own), low),
        in_specs=[pl.BlockSpec(memory_space=pltpu.HBM)] * 8,
        out_specs=pl.BlockSpec(memory_space=pltpu.VMEM),
        scratch_shapes=[
            vmem((tok_dev, width), low),
            vmem((tok_dev, cot_width), low),
            vmem((1, examples), whole),
            vmem((1, width), whole),
            vmem((1, cot_width), whole),
            vmem((1, features), whole),
            vmem((1, features), whole),
            vmem((2, row_count, tok_dev, width), low),
            vmem((2, tok_dev, cot_width), low),
            vmem((row_count * width, row_count * half), low),
            vmem((2, tok_dev, row_count * half), wide),
            vmem((2 * tok_dev, row_count * half), low),
            vmem((2 * tok_dev, row_count * half), low),
            vmem((row_count, groups, examples // groups, half), wide),
            vmem((row_count, others, examples // groups, half), low),
            vmem((row_count, others, examples // groups, half), low),
            vmem((last, others, examples // groups, half), low),
            vmem((examples // groups, half), wide),
            vmem((last, examples // groups, half), low),
            vmem((last, examples // groups, half), low),
            vmem((row_count, 2, owned, own), wide),
            vmem((row_count, owned, own), wide),
            vmem((last, owned, own), low),
            vmem((last, owned, own), low),
            vmem((row_count, half, own), low),
            dma((7,)),
            dma((row_count,)),
            dma((last,)),
            dma((last,)),
            dma((row_count,)),
            dma((row_count,)),
            dma,
            dma,
            dma((row_count, others)),
            dma((row_count, others)),
            dma((last, others)),
            dma((last, others)),
            dma((last,)),
            dma((last,)),
            dma((row_count,)),
            dma((row_count,)),
            dma((last,)),
            dma((last,)),
        ],
        compiler_params=pltpu.CompilerParams(
            collective_id=0, has_side_effects=True, vmem_limit_bytes=48 * 1024 * 1024
        ),
        name="features_and_scores",
    )(*[pltpu.with_memory_space_constraint(operand, pltpu.HBM) for operand in operands])


def local(hidden_acts, cotangent, lengths, row_signs, col_signs, feat_row, feat_col, inverse_rows):
    row_count = lax.axis_size("rows")
    ex_count = lax.axis_size("ex")
    tok_dev, width = hidden_acts.shape
    cot_width = cotangent.shape[1]
    features = feat_row.shape[0]
    examples = lengths.shape[0]
    own = features // row_count
    owned = examples // ex_count
    norm_scale = 1.0 / math.sqrt(width * row_count * col_signs.shape[0])
    operands = (
        hidden_acts,
        cotangent,
        lengths.reshape(1, -1),
        row_signs.reshape(1, -1),
        col_signs.reshape(1, -1),
        feat_row.reshape(1, -1),
        feat_col.reshape(1, -1),
        inverse_rows,
    )
    if (
        ex_count % 2 == 0
        and row_count in (2, 4, 8)
        and own % 256 == 0
        and cot_width % 128 == 0
        and width % 128 == 0
        and tok_dev % 16 == 0
        and owned % 8 == 0
        and features * (width * row_count + cot_width + own) <= 32 * 1024 * 1024
    ):
        return pair_call(row_count, ex_count, norm_scale, operands)
    if cot_width % 128 != 0:
        col_signs = lax.dynamic_slice(col_signs, (lax.axis_index("rows") * cot_width,), (cot_width,))
    vmem = pl.BlockSpec(memory_space=pltpu.VMEM)
    others = max(row_count - 1, 1)
    dma = pltpu.SemaphoreType.DMA
    return pl.pallas_call(
        functools.partial(kernel, row_count, ex_count, norm_scale),
        out_shape=jax.ShapeDtypeStruct((owned, own), jnp.bfloat16),
        in_specs=[vmem] * 7 + [pl.BlockSpec(memory_space=pl.ANY)],
        out_specs=vmem,
        scratch_shapes=[
            pltpu.VMEM((row_count, tok_dev, width), jnp.bfloat16),
            pltpu.VMEM((tok_dev, cot_width), jnp.bfloat16),
            pltpu.VMEM((row_count, tok_dev, own), jnp.float32),
            pltpu.VMEM((row_count, ex_count, owned, own), jnp.float32),
            pltpu.VMEM((row_count, max(ex_count - 1, 1), owned, own), jnp.float32),
            pltpu.VMEM((others, owned, own), jnp.bfloat16),
            pltpu.VMEM((others, owned, own), jnp.bfloat16),
            pltpu.VMEM((others, owned, own), jnp.bfloat16),
            pltpu.VMEM((others, owned, own), jnp.bfloat16),
            pltpu.VMEM((row_count, own, own), jnp.bfloat16),
            pltpu.VMEM((owned, own), jnp.float32),
            dma((row_count,)),
            dma((others,)),
            dma((others,)),
            dma((row_count, max(ex_count - 1, 1))),
            dma((row_count, max(ex_count - 1, 1))),
            dma((others,)),
            dma((others,)),
            dma((others,)),
            dma((others,)),
        ],
        compiler_params=pltpu.CompilerParams(
            collective_id=0, has_side_effects=True, vmem_limit_bytes=60 * 1024 * 1024
        ),
        name="features_and_scores",
    )(
        hidden_acts,
        cotangent,
        lengths.reshape(1, -1),
        row_signs.reshape(1, -1),
        col_signs.reshape(1, -1),
        feat_row.reshape(1, -1),
        feat_col.reshape(1, -1),
        inverse_rows,
    )


def solution(mesh):
    placed = (
        P(("parts", "ex"), "rows"),
        P(("parts", "ex"), "rows"),
        P("parts"),
        P("rows"),
        P(),
        P(),
        P(),
        P("rows", None),
    )
    return jax.shard_map(
        local, mesh=mesh, in_specs=placed, out_specs=P(("parts", "ex"), "rows"), check_vma=False
    )
```
